512 devices in a mesh: dp: 2 (over y_lo), ctx: 32 (over y_hi, x, core), tensor: 8 (over z).
Axes of the slice: x: 4, y: 8 (y_hi: 4, y_lo: 2; y = y_hi * 2 + y_lo), z: 8, core: 2. Of those that a mesh axis runs over, the one named last changes fastest.
Arguments:
- queries: bfloat16 [8192, 8192], P(('dp', 'ctx'), 'tensor'), parts along dimension 0, may hold values from -6 to 6
- keys: bfloat16 [8192, 1024], P(('dp', 'ctx'), 'tensor'), parts along dimension 0, may hold values from -6 to 6
- values: bfloat16 [8192, 1024], P(('dp', 'ctx'), 'tensor'), parts along dimension 0, may hold values from -6 to 6
- attn_out: bfloat16 [8192, 8192], P(('dp', 'ctx'), 'tensor'), parts along dimension 0, may hold values from -6 to 6
- grad_out: bfloat16 [8192, 8192], P(('dp', 'ctx'), 'tensor'), parts along dimension 0, may hold values from -6 to 6
- log_norm: float32 [64, 8192], P('tensor', ('dp', 'ctx')), parts along dimension 1, may hold values from 3 to 6
- doc_lengths: int32 [32], P('dp'), parts along dimension 0, may hold values from 1 to 1024, 4096 in all
- block_order: int32 [128], P('dp'), parts along dimension 0, may hold values from 0 to 63, each once
Outputs:
- grad_queries: bfloat16 [8192, 8192], P(('dp', 'ctx'), 'tensor'), parts along dimension 0
- key_gradient_rows: bfloat16 [8192, 1024], P(('dp', 'ctx'), 'tensor'), parts along dimension 0
- value_gradient_rows: bfloat16 [8192, 1024], P(('dp', 'ctx'), 'tensor'), parts along dimension 0
The draws below stay inside these ranges and needn't reach their ends.
There are 2 independent parts, one for each index of `dp`. The reference program is written for one: setup_inputs(seed, part) draws one part's arguments, and reference() takes and returns one part's arrays. A program takes and returns all parts, laid end to end along the dimension named above; each array names one. Nothing has to cross between parts.
Inputs may be any that keep to these rules, and one draw needn't show every extreme that they name: `doc_lengths`: document lengths in sequence order; they sum to 4096 and the largest is exactly 1024. `block_order`: each of the 64 blocks of 64 positions appears once.
All inputs are finite; a program needn't handle non-finite values.
Results may differ from the reference program's by a relative error of at most 0.0049.
Values may be sent and summed in bfloat16 or wider, within the bound.
No kernel may reach another device: no remote copies, remote signals or barrier semaphores. Data moves between devices by JAX's collectives and lax.ppermute only.
A program may use at most 64 MiB of HBM per device.

```python
import math
import jax
import jax.numpy as jnp
import numpy as np
from jax import lax

QUERY_HEADS = 64
KEY_VALUE_HEADS = 8
HEAD_SIZE = 128
DOCS = 16
PACKED_POSITIONS = 4096
BLOCK = 64
NBLK = 64


def level_of(key, shape, shards, low, high):
    def one(axis_at, parts):
        draws = jax.random.uniform(jax.random.fold_in(jax.random.fold_in(key, 6), axis_at), (parts,), jnp.float32, low / len(shards), high / len(shards))
        return jnp.repeat(jnp.exp(draws), shape[axis_at] // parts).reshape((-1,) + (1,) * (len(shape) - axis_at - 1))

    loudness = one(*shards[0])
    for cut in shards[1:]:
        loudness = loudness * one(*cut)
    return loudness


def length_profile(number_of, total, most, slope):
    loads = [(1 << 20) // math.isqrt(standing ** slope) + 1 for standing in range(2, number_of + 1)]
    rest, holding = total - most - (number_of - 1), [1] * (number_of - 1)
    while rest > 0:
        candidates = [i for i in range(number_of - 1) if holding[i] < most]
        pool, remaining = sum([loads[i] for i in candidates]), rest
        for i in candidates:
            extra = min(most - holding[i], max(1, remaining * loads[i] // pool), rest)
            holding[i] = holding[i] + extra
            rest = rest - extra
    return np.array([most] + holding)


def uneven_parts(rng, amount, total, bound, slope):
    if amount == 2:
        one = jax.random.randint(rng, (), max(1, total - bound), min(bound, total - 1) + 1)
        return jnp.stack([one, total - one])
    sizes = jnp.asarray(length_profile(amount, total, bound, slope), jnp.int32)
    twos = (amount - 1) // 2
    source_of, sink = sizes[1:1 + 2 * twos:2], sizes[2:2 + 2 * twos:2]
    margin = jnp.minimum(source_of - 1, bound - sink)
    passed = jax.random.randint(jax.random.fold_in(rng, 1), (twos,), 0, 1 << 20) % (margin + 1)
    sizes = sizes.at[1:1 + 2 * twos:2].set(source_of - passed).at[2:2 + 2 * twos:2].set(sink + passed)
    return sizes[jax.random.permutation(jax.random.fold_in(rng, 2), amount)]


def centred(rng, shape, scale, most, cuts=(), kind=jnp.bfloat16):
    loudness = level_of(rng, shape, cuts, -0.22, 0.18) if cuts else 1.0
    array = jax.random.normal(rng, shape, jnp.float32) * scale * loudness
    return jnp.minimum(jnp.maximum(array, -most), most).astype(kind)


def setup_inputs(seed: int = 0, part: int = 0) -> dict:
    key_list = jax.random.split(jax.random.key(seed), 9)
    own_keys = jax.random.split(jax.random.fold_in(key_list[8], part), 9)
    queries = centred(own_keys[0], (PACKED_POSITIONS, QUERY_HEADS * HEAD_SIZE), 1.0, 6.0, ((0, 32), (1, 8)))
    keys = centred(own_keys[1], (PACKED_POSITIONS, KEY_VALUE_HEADS * HEAD_SIZE), 1.0, 6.0, ((0, 32), (1, 8)))
    values = centred(own_keys[2], (PACKED_POSITIONS, KEY_VALUE_HEADS * HEAD_SIZE), 1.0, 6.0, ((0, 32), (1, 8)))
    attn_out = centred(own_keys[3], (PACKED_POSITIONS, QUERY_HEADS * HEAD_SIZE), 1.0, 6.0, ((0, 32), (1, 8)))
    grad_out = centred(own_keys[4], (PACKED_POSITIONS, QUERY_HEADS * HEAD_SIZE), 1.0, 6.0, ((0, 32), (1, 8)))
    log_norm = jnp.clip(3.0 + 3.0 * jax.random.uniform(own_keys[5], (QUERY_HEADS, PACKED_POSITIONS), jnp.float32) ** level_of(own_keys[5], (QUERY_HEADS, PACKED_POSITIONS), ((0, 8), (1, 32)), -0.2, 0.2), 3.0, 6.0)
    doc_lengths = uneven_parts(own_keys[6], DOCS, PACKED_POSITIONS, 4 * PACKED_POSITIONS // DOCS, 2).astype(jnp.int32)
    block_order = jax.random.permutation(own_keys[7], NBLK).astype(jnp.int32)
    return dict(queries=queries, keys=keys, values=values, attn_out=attn_out, grad_out=grad_out, log_norm=log_norm, doc_lengths=doc_lengths, block_order=block_order)


def doc_layout(doc_lengths, block_order):
    seq_index = jnp.arange(PACKED_POSITIONS, dtype=jnp.int32)
    position = block_order[seq_index // BLOCK].astype(jnp.int32) * BLOCK + seq_index % BLOCK
    doc_ends = jnp.cumsum(doc_lengths).astype(jnp.int32)
    doc_ids = lax.optimization_barrier(jnp.sum((position[:, None] >= doc_ends[None, :]).astype(jnp.int32), axis=1))
    return (position, doc_ids)

def reference(queries, keys, values, attn_out, grad_out, log_norm, doc_lengths, block_order):
    position, doc_ids = doc_layout(doc_lengths, block_order)
    allowed = (doc_ids[:, None] == doc_ids[None, :]) & (position[None, :] <= position[:, None])
    query_group_width = QUERY_HEADS // KEY_VALUE_HEADS
    score_scale = 1.0 / math.sqrt(HEAD_SIZE)

    def one_head(head_index):
        group_index = head_index // query_group_width
        query_head = lax.dynamic_slice_in_dim(queries, head_index * HEAD_SIZE, HEAD_SIZE, 1)
        out_head = lax.dynamic_slice_in_dim(attn_out, head_index * HEAD_SIZE, HEAD_SIZE, 1)
        grad_head = lax.dynamic_slice_in_dim(grad_out, head_index * HEAD_SIZE, HEAD_SIZE, 1)
        key_head = lax.dynamic_slice_in_dim(keys, group_index * HEAD_SIZE, HEAD_SIZE, 1)
        value_head = lax.dynamic_slice_in_dim(values, group_index * HEAD_SIZE, HEAD_SIZE, 1)
        norm_row = lax.dynamic_index_in_dim(log_norm, head_index, 0, keepdims=False)
        scores = jnp.dot(query_head, key_head.T, preferred_element_type=jnp.float32) * score_scale
        weights = jnp.where(allowed, jnp.exp(scores - norm_row[:, None]), jnp.zeros_like(scores))
        grad_weights = jnp.dot(grad_head, value_head.T, preferred_element_type=jnp.float32)
        out_dot = lax.optimization_barrier(jnp.sum(grad_head.astype(jnp.float32) * out_head.astype(jnp.float32), axis=1))
        grad_scores = (weights * (grad_weights - out_dot[:, None]) * score_scale).astype(jnp.bfloat16)
        weights_bf = weights.astype(jnp.bfloat16)
        grad_query = jnp.dot(grad_scores, key_head, preferred_element_type=jnp.float32).astype(jnp.bfloat16)
        grad_key = jnp.dot(grad_scores.T, query_head, preferred_element_type=jnp.float32)
        grad_value = jnp.dot(weights_bf.T, grad_head, preferred_element_type=jnp.float32)
        return (grad_query, grad_key, grad_value)
    all_query, every_key_row, every_value_row = lax.map(one_head, jnp.arange(QUERY_HEADS, dtype=jnp.int32))
    grad_queries = jnp.transpose(all_query, (1, 0, 2)).reshape(PACKED_POSITIONS, QUERY_HEADS * HEAD_SIZE)
    key_gradient_sum = every_key_row.reshape(KEY_VALUE_HEADS, query_group_width, PACKED_POSITIONS, HEAD_SIZE).sum(axis=1)
    value_gradient_sum = every_value_row.reshape(KEY_VALUE_HEADS, query_group_width, PACKED_POSITIONS, HEAD_SIZE).sum(axis=1)
    key_gradient_rows = jnp.transpose(key_gradient_sum, (1, 0, 2)).reshape(PACKED_POSITIONS, KEY_VALUE_HEADS * HEAD_SIZE).astype(jnp.bfloat16)
    value_gradient_rows = jnp.transpose(value_gradient_sum, (1, 0, 2)).reshape(PACKED_POSITIONS, KEY_VALUE_HEADS * HEAD_SIZE).astype(jnp.bfloat16)
    return (grad_queries, key_gradient_rows, value_gradient_rows)
```

```python
import math

import jax
import jax.numpy as jnp
from jax import lax
from jax.experimental import pallas as pl
from jax.experimental.pallas import tpu as pltpu
from jax.sharding import Mesh
from jax.sharding import PartitionSpec as P

HEADS = 8
HEAD = 128
BLOCK = 64
LANES = HEADS * BLOCK
SCALE = 1.0 / math.sqrt(HEAD)
LOG2E = math.log2(math.e)
CTX = ("yh", "x", "core")
CHIPS = ("yh", "x")
NT = (((1,), (1,)), ((), ()))
TN = (((0,), (0,)), ((), ()))


def attention_terms(
    from_ref, upto_ref, held_ref, place_ref,
    q_ref, q2_ref, do_ref, do2_ref, rows_f_ref, rows_i_ref, kv_ref,
    dq_ref, dq2_ref, dkv_ref, acc_ref, dqt_ref,
):
    acc_ref[...] = jnp.zeros_like(acc_ref)
    heads = range(HEADS)
    for b in range(4):
        rows = pl.ds((b % 2) * BLOCK, BLOCK)
        qs, dos, out = (q_ref, do_ref, dq_ref) if b < 2 else (q2_ref, do2_ref, dq2_ref)
        q = jnp.concatenate([qs[rows, h * HEAD : (h + 1) * HEAD] for h in heads], 0)
        do = jnp.concatenate([dos[rows, h * HEAD : (h + 1) * HEAD] for h in heads], 0)
        norm = rows_f_ref[2 * b : 2 * b + 1, :]
        dot = rows_f_ref[2 * b + 1 : 2 * b + 2, :]
        first = rows_i_ref[2 * b : 2 * b + 1, :]
        own = rows_i_ref[2 * b + 1 : 2 * b + 2, :]
        start, stop = from_ref[b], upto_ref[b]
        dqt_ref[...] = jnp.zeros_like(dqt_ref)

        def step(c, carry, q=q, do=do, norm=norm, dot=dot, first=first, own=own, start=start):
            j = start + 2 * c
            a0 = pl.multiple_of(place_ref[j], BLOCK)
            a1 = pl.multiple_of(place_ref[j + 1], BLOCK)
            k = jnp.concatenate([kv_ref[pl.ds(a0, BLOCK), :], kv_ref[pl.ds(a1, BLOCK), :]], 0)
            v = jnp.concatenate(
                [kv_ref[pl.ds(a0 + 128, BLOCK), :], kv_ref[pl.ds(a1 + 128, BLOCK), :]], 0
            )
            s = lax.dot_general(k, q, NT, preferred_element_type=jnp.float32)
            dp = lax.dot_general(v, do, NT, preferred_element_type=jnp.float32)
            lane = lax.broadcasted_iota(jnp.int32, (BLOCK, LANES), 0)
            pos = jnp.concatenate([lane + held_ref[j] * BLOCK, lane + held_ref[j + 1] * BLOCK], 0)
            ok = (pos >= first) & (pos <= own)
            w = jnp.where(ok, jnp.exp2(s * (SCALE * LOG2E) - norm), 0.0)
            ds = (w * (dp - dot) * SCALE).astype(jnp.bfloat16)
            wb = w.astype(jnp.bfloat16)
            dv = jnp.dot(wb, do, preferred_element_type=jnp.float32)
            dk = jnp.dot(ds, q, preferred_element_type=jnp.float32)
            dqt_ref[...] += lax.dot_general(k, ds, TN, preferred_element_type=jnp.float32)
            acc_ref[pl.ds(a0, BLOCK), :] += dk[:BLOCK]
            acc_ref[pl.ds(a1, BLOCK), :] += dk[BLOCK:]
            acc_ref[pl.ds(a0 + 128, BLOCK), :] += dv[:BLOCK]
            acc_ref[pl.ds(a1 + 128, BLOCK), :] += dv[BLOCK:]
            return carry

        lax.fori_loop(0, (stop - start + 1) // 2, step, 0)
        dq = dqt_ref[...].T.astype(out.dtype)
        for h in heads:
            out[rows, h * HEAD : (h + 1) * HEAD] = dq[h * BLOCK : (h + 1) * BLOCK]
    dkv_ref[...] = acc_ref[...].astype(jnp.bfloat16)


def lanes(x):
    return x.transpose(0, 2, 1).reshape(2, LANES)


def on_device(queries, keys, values, attn_out, grad_out, log_norm, doc_lengths, block_order):
    rows = queries.shape[0]
    nblk = block_order.shape[0]
    nheld = nblk // 2
    me, core = lax.axis_index(CTX), lax.axis_index("core")
    kv = jnp.concatenate([keys, values], 0)
    kv = lax.all_to_all(jnp.broadcast_to(kv, (16,) + kv.shape), CHIPS, 0, 0, tiled=True)

    swap = [(0, 1), (1, 0)]
    q2 = lax.ppermute(queries, "core", swap)
    do2 = lax.ppermute(grad_out, "core", swap)
    gh = grad_out.reshape(2, BLOCK, HEADS, HEAD).astype(jnp.float32)
    oh = attn_out.reshape(2, BLOCK, HEADS, HEAD).astype(jnp.float32)
    out_dot = lanes(jnp.sum(gh * oh, axis=3))
    norm = (log_norm * LOG2E).reshape(HEADS, 2, BLOCK).transpose(1, 0, 2).reshape(2, LANES)
    rows_f = jnp.stack([norm, out_dot], axis=1).reshape(4, LANES)
    rows_f = jnp.concatenate([rows_f, lax.ppermute(rows_f, "core", swap)], 0)

    docs = doc_lengths.shape[0]
    upto = jnp.arange(docs)[:, None] >= jnp.arange(docs)[None, :]
    ends = jnp.sum(jnp.where(upto, doc_lengths[None, :], 0), axis=1)
    blocks = jnp.arange(nblk, dtype=jnp.int32)
    held_here = (blocks // 2) % 2 == core
    place = (blocks // 4) * (2 * rows) + (blocks % 2) * BLOCK
    before = held_here[None, :] & (block_order[None, :] < block_order[:, None])
    rank = jnp.sum(before.astype(jnp.int32), axis=1)
    slots = jnp.arange(nheld + 8, dtype=jnp.int32)
    hit = held_here[None, :] & (rank[None, :] == slots[:, None])
    held = jnp.sum(jnp.where(hit, block_order[None, :], 0), axis=1)
    held = jnp.where(slots < nheld, held, nblk)
    place = jnp.sum(jnp.where(hit, place[None, :], 0), axis=1)
    mine = jnp.concatenate(
        [
            lax.dynamic_slice_in_dim(block_order, me * 2, 2),
            lax.dynamic_slice_in_dim(block_order, (me + 1 - 2 * core) * 2, 2),
        ]
    )
    pos = mine[:, None] * BLOCK + jnp.arange(BLOCK, dtype=jnp.int32)[None, :]
    first = jnp.max(jnp.where(ends[None, None, :] <= pos[:, :, None], ends[None, None, :], 0), axis=2)
    lo = first[:, 0] // BLOCK
    begin = jnp.sum((held[None, :] < lo[:, None]).astype(jnp.int32), axis=1)
    until = jnp.sum((held[None, :] <= mine[:, None]).astype(jnp.int32), axis=1)
    rows_i = jnp.tile(jnp.stack([first, pos], axis=1), (1, 1, HEADS)).reshape(8, LANES)

    vmem = pl.BlockSpec(memory_space=pltpu.VMEM)
    smem = pl.BlockSpec(memory_space=pltpu.SMEM)
    total = 2 * nheld * BLOCK
    dq, dq2, dkv = pl.pallas_call(
        attention_terms,
        out_shape=(
            jax.ShapeDtypeStruct(queries.shape, jnp.float32),
            jax.ShapeDtypeStruct(queries.shape, jnp.bfloat16),
            jax.ShapeDtypeStruct((total, HEAD), jnp.bfloat16),
        ),
        in_specs=[smem] * 4 + [vmem] * 7,
        out_specs=(vmem,) * 3,
        scratch_shapes=[
            pltpu.VMEM((total, HEAD), jnp.float32),
            pltpu.VMEM((HEAD, LANES), jnp.float32),
        ],
        compiler_params=pltpu.CompilerParams(vmem_limit_bytes=32 << 20),
        name="attention_terms",
    )(begin, until, held, place, queries, q2, grad_out, do2, rows_f, rows_i, kv.reshape(total, HEAD))

    got = lax.all_to_all(dkv.reshape(16, 2 * rows, HEAD), CHIPS, 0, 0, tiled=True)
    other = lax.ppermute(dq2, "core", swap)
    grad_q = (dq + other.astype(jnp.float32)).astype(jnp.bfloat16)
    both = jnp.sum(got.astype(jnp.float32), axis=0).astype(jnp.bfloat16)
    return grad_q, both[:rows], both[rows:]


def solution(mesh):
    parts = Mesh(mesh.devices.reshape(2, 4, 4, 2, 8), ("dp", "yh", "x", "core", "tensor"))
    seq = ("dp",) + CTX
    wide = P(seq, "tensor")
    return jax.shard_map(
        on_device,
        mesh=parts,
        in_specs=(wide,) * 5 + (P("tensor", seq), P("dp"), P("dp")),
        out_specs=(wide, wide, wide),
        check_vma=False,
    )
```

```python
import math

import jax
import jax.numpy as jnp
from jax import lax
from jax.experimental import pallas as pl
from jax.experimental.pallas import tpu as pltpu
from jax.sharding import Mesh
from jax.sharding import PartitionSpec as P

HEADS = 8
HEAD = 128
BLOCK = 64
LANES = HEADS * BLOCK
SCALE = 1.0 / math.sqrt(HEAD)
LOG2E = math.log2(math.e)
CTX = ("yh", "xh", "xl", "core")
KEEPERS = ("yh", "xh")
NEXT = ("xh", "xl", "core")
NT = (((1,), (1,)), ((), ()))
TN = (((0,), (0,)), ((), ()))


def pack_rows(norm_ref, q_ref, do_ref, o_ref, out_ref):
    rows = q_ref.shape[0]
    out_ref[:rows] = q_ref[...]
    out_ref[rows : 2 * rows] = do_ref[...]
    ones = jnp.ones((8, HEAD), jnp.float32)
    dots = []
    for b in range(2):
        at = slice(b * BLOCK, (b + 1) * BLOCK)
        prod = jnp.concatenate(
            [
                do_ref[at, h * HEAD : (h + 1) * HEAD].astype(jnp.float32)
                * o_ref[at, h * HEAD : (h + 1) * HEAD].astype(jnp.float32)
                for h in range(HEADS)
            ],
            0,
        )
        dots.append(
            lax.dot_general(
                ones, prod, NT, precision=lax.Precision.HIGHEST, preferred_element_type=jnp.float32
            )[:1]
        )
    parts = []
    for x in (norm_ref[...], jnp.concatenate(dots, 1)):
        for _ in range(3):
            term = x.astype(jnp.bfloat16).astype(jnp.float32)
            parts.append(term)
            x = x - term
    parts.append(jnp.zeros((10, 2 * LANES), jnp.float32))
    out_ref[2 * rows :] = jnp.concatenate(parts, 0).astype(jnp.bfloat16)


def attention_terms(
    from_ref, upto_ref, held_ref, place_ref, rows_i_ref, p0_ref, p1_ref, p2_ref, p3_ref, kv_ref,
    dq0_ref, dq2_ref, sib_ref, dkv_ref, acc_ref, dqt_ref,
):
    acc_ref[...] = jnp.zeros_like(acc_ref)
    heads = range(HEADS)
    nrow = dq0_ref.shape[0]
    outs = (dq0_ref, sib_ref.at[:nrow], dq2_ref, sib_ref.at[nrow:])
    for g, (p_ref, out) in enumerate(zip((p0_ref, p1_ref, p2_ref, p3_ref), outs)):
        more = p_ref[2 * nrow :, :].astype(jnp.float32)
        norms = more[0:1] + more[1:2] + more[2:3]
        dots = more[3:4] + more[4:5] + more[5:6]
        for i in range(2):
            b = 2 * g + i
            at = slice(i * BLOCK, (i + 1) * BLOCK)
            at2 = slice(nrow + i * BLOCK, nrow + (i + 1) * BLOCK)
            q = jnp.concatenate([p_ref[at, h * HEAD : (h + 1) * HEAD] for h in heads], 0)
            do = jnp.concatenate([p_ref[at2, h * HEAD : (h + 1) * HEAD] for h in heads], 0)
            norm = norms[:, i * LANES : (i + 1) * LANES]
            dot = dots[:, i * LANES : (i + 1) * LANES]
            first = rows_i_ref[2 * b : 2 * b + 1, :]
            own = rows_i_ref[2 * b + 1 : 2 * b + 2, :]
            start, stop = from_ref[b], upto_ref[b]
            dqt_ref[...] = jnp.zeros_like(dqt_ref)

            def step(c, carry, q=q, do=do, norm=norm, dot=dot, first=first, own=own, start=start):
                j = start + 2 * c
                a0 = pl.multiple_of(place_ref[j], BLOCK)
                a1 = pl.multiple_of(place_ref[j + 1], BLOCK)
                k = jnp.concatenate([kv_ref[pl.ds(a0, BLOCK), :], kv_ref[pl.ds(a1, BLOCK), :]], 0)
                v = jnp.concatenate(
                    [kv_ref[pl.ds(a0 + 128, BLOCK), :], kv_ref[pl.ds(a1 + 128, BLOCK), :]], 0
                )
                s = lax.dot_general(k, q, NT, preferred_element_type=jnp.float32)
                dp = lax.dot_general(v, do, NT, preferred_element_type=jnp.float32)
                lane = lax.broadcasted_iota(jnp.int32, (BLOCK, LANES), 0)
                pos = jnp.concatenate(
                    [lane + held_ref[j] * BLOCK, lane + held_ref[j + 1] * BLOCK], 0
                )
                ok = (pos >= first) & (pos <= own)
                w = jnp.where(ok, jnp.exp2(s * (SCALE * LOG2E) - norm), 0.0)
                ds = (w * (dp - dot) * SCALE).astype(jnp.bfloat16)
                wb = w.astype(jnp.bfloat16)
                dv = jnp.dot(wb, do, preferred_element_type=jnp.float32)
                dk = jnp.dot(ds, q, preferred_element_type=jnp.float32)
                dqt_ref[...] += lax.dot_general(k, ds, TN, preferred_element_type=jnp.float32)
                acc_ref[pl.ds(a0, BLOCK), :] += dk[:BLOCK]
                acc_ref[pl.ds(a1, BLOCK), :] += dk[BLOCK:]
                acc_ref[pl.ds(a0 + 128, BLOCK), :] += dv[:BLOCK]
                acc_ref[pl.ds(a1 + 128, BLOCK), :] += dv[BLOCK:]
                return carry

            lax.fori_loop(0, (stop - start + 1) // 2, step, 0)
            dq = dqt_ref[...].T.astype(out.dtype)
            for h in heads:
                out[at, h * HEAD : (h + 1) * HEAD] = dq[h * BLOCK : (h + 1) * BLOCK]
    dkv_ref[...] = acc_ref[...].astype(jnp.bfloat16)


def on_device(queries, keys, values, attn_out, grad_out, log_norm, doc_lengths, block_order):
    rows = queries.shape[0]
    nblk = block_order.shape[0]
    nheld = nblk // 4
    yh, xh, xl, core = (lax.axis_index(a) for a in CTX)
    x = 2 * xh + xl
    vmem = pl.BlockSpec(memory_space=pltpu.VMEM)
    smem = pl.BlockSpec(memory_space=pltpu.SMEM)

    kv = jnp.concatenate([keys, values], 0)
    kv = lax.all_to_all(jnp.broadcast_to(kv, (8,) + kv.shape), KEEPERS, 0, 0, tiled=True)

    norm = (log_norm * LOG2E).reshape(HEADS, 2, BLOCK).transpose(1, 0, 2).reshape(1, 2 * LANES)
    p0 = pl.pallas_call(
        pack_rows,
        out_shape=jax.ShapeDtypeStruct((2 * rows + 16, queries.shape[1]), jnp.bfloat16),
        in_specs=[vmem] * 4,
        out_specs=vmem,
        compiler_params=pltpu.CompilerParams(vmem_limit_bytes=16 << 20),
        name="pack_rows",
    )(norm, queries, grad_out, attn_out)
    swap = [(0, 1), (1, 0)]
    there = [(2 * ((i + 1) % 4), 2 * i) for i in range(4)]
    there += [(2 * i + 1, 2 * ((i + 1) % 4) + 1) for i in range(4)]
    back = [(j, i) for i, j in there]
    p1 = lax.ppermute(p0, "core", swap)
    p2 = lax.ppermute(p0, NEXT, there)
    p3 = lax.ppermute(p2, "core", swap)

    docs = doc_lengths.shape[0]
    upto = jnp.arange(docs)[:, None] >= jnp.arange(docs)[None, :]
    ends = jnp.sum(jnp.where(upto, doc_lengths[None, :], 0), axis=1)
    blocks = jnp.arange(nblk, dtype=jnp.int32)
    held_here = ((blocks // 2) % 2 == core) & ((blocks // 4) % 2 == xl)
    place = (blocks // 8) * (2 * rows) + (blocks % 2) * BLOCK
    before = held_here[None, :] & (block_order[None, :] < block_order[:, None])
    rank = jnp.sum(before.astype(jnp.int32), axis=1)
    slots = jnp.arange(nheld + 8, dtype=jnp.int32)
    hit = held_here[None, :] & (rank[None, :] == slots[:, None])
    held = jnp.sum(jnp.where(hit, block_order[None, :], 0), axis=1)
    held = jnp.where(slots < nheld, held, nblk)
    place = jnp.sum(jnp.where(hit, place[None, :], 0), axis=1)
    turn = 1 - 2 * core
    owners = jnp.stack(
        [
            2 * x + core,
            2 * x + 1 - core,
            2 * ((x + turn) % 4) + core,
            2 * ((x - turn) % 4) + 1 - core,
        ]
    ) + 8 * yh
    stored = (2 * owners[:, None] + jnp.arange(2)[None, :]).reshape(8)
    mine = jnp.sum(jnp.where(stored[:, None] == blocks[None, :], block_order[None, :], 0), axis=1)
    pos = mine[:, None] * BLOCK + jnp.arange(BLOCK, dtype=jnp.int32)[None, :]
    first = jnp.max(jnp.where(ends[None, None, :] <= pos[:, :, None], ends[None, None, :], 0), axis=2)
    lo = first[:, 0] // BLOCK
    begin = jnp.sum((held[None, :] < lo[:, None]).astype(jnp.int32), axis=1)
    until = jnp.sum((held[None, :] <= mine[:, None]).astype(jnp.int32), axis=1)
    rows_i = jnp.tile(jnp.stack([first, pos], axis=1), (1, 1, HEADS)).reshape(16, LANES)

    total = 2 * nheld * BLOCK
    dq0, dq2, sib, dkv = pl.pallas_call(
        attention_terms,
        out_shape=(
            jax.ShapeDtypeStruct(queries.shape, jnp.float32),
            jax.ShapeDtypeStruct(queries.shape, jnp.float32),
            jax.ShapeDtypeStruct((2 * rows, queries.shape[1]), jnp.bfloat16),
            jax.ShapeDtypeStruct((total, HEAD), jnp.bfloat16),
        ),
        in_specs=[smem] * 4 + [vmem] * 6,
        out_specs=(vmem,) * 4,
        scratch_shapes=[
            pltpu.VMEM((total, HEAD), jnp.float32),
            pltpu.VMEM((HEAD, LANES), jnp.float32),
        ],
        compiler_params=pltpu.CompilerParams(vmem_limit_bytes=32 << 20),
        name="attention_terms",
    )(begin, until, held, place, rows_i, p0, p1, p2, p3, kv.reshape(total, HEAD))

    got = lax.all_to_all(dkv.reshape(8, 2 * rows, HEAD), KEEPERS, 0, 0, tiled=True)
    sib = lax.ppermute(sib, "core", swap).astype(jnp.float32)
    far = lax.ppermute((dq2 + sib[rows:]).astype(jnp.bfloat16), NEXT, back)
    grad_q = (dq0 + sib[:rows] + far.astype(jnp.float32)).astype(jnp.bfloat16)
    both = jnp.sum(got.astype(jnp.float32), axis=0).astype(jnp.bfloat16)
    return grad_q, both[:rows], both[rows:]


def solution(mesh):
    parts = Mesh(
        mesh.devices.reshape(2, 4, 2, 2, 2, 8), ("dp", "yh", "xh", "xl", "core", "tensor")
    )
    seq = ("dp",) + CTX
    wide = P(seq, "tensor")
    return jax.shard_map(
        on_device,
        mesh=parts,
        in_specs=(wide,) * 5 + (P("tensor", seq), P("dp"), P("dp")),
        out_specs=(wide, wide, wide),
        check_vma=False,
    )
```

```python
import math

import jax
import jax.numpy as jnp
from jax import lax
from jax.experimental import pallas as pl
from jax.experimental.pallas import tpu as pltpu
from jax.sharding import Mesh
from jax.sharding import PartitionSpec as P

HEADS = 8
HEAD = 128
BLOCK = 64
ROWS = 2 * BLOCK
WIDTH = HEADS * HEAD
LANES = HEADS * BLOCK
EXTRA = 16
PEERS = 8
SLOTS = 72
SCALE = 1.0 / math.sqrt(HEAD)
LOG2E = math.log2(math.e)
CTX = ("yh", "xh", "xl", "core")
KEEPERS = ("yh", "xh")
NEXT = ("xh", "xl", "core")
NT = (((1,), (1,)), ((), ()))
TN = (((0,), (0,)), ((), ()))
VMEM = pl.BlockSpec(memory_space=pltpu.VMEM)
SMEM = pl.BlockSpec(memory_space=pltpu.SMEM)
HBM = pl.BlockSpec(memory_space=pltpu.HBM)


def head(h):
    return slice(h * HEAD, (h + 1) * HEAD)


def in_hbm(x):
    return pltpu.with_memory_space_constraint(x, pltpu.HBM)


def call(kernel, out, ins, outs, *args, scratch=(), limit=16):
    return pl.pallas_call(
        kernel,
        out_shape=out,
        in_specs=ins,
        out_specs=outs,
        scratch_shapes=scratch,
        compiler_params=pltpu.CompilerParams(vmem_limit_bytes=limit << 20),
        name=kernel.__name__,
    )(*args)


def terms_of(x):
    parts = []
    for _ in range(3):
        term = x.astype(jnp.bfloat16).astype(jnp.float32)
        parts.append(term)
        x = x - term
    return parts


def pack(
    k_ref, v_ref, q_ref, do_ref, o_ref, norm_ref, kv_ref, out_ref, kv_buf, o_buf, sem, kv_sem
):
    reads = [
        pltpu.make_async_copy(k_ref, kv_buf.at[:ROWS], sem.at[0]),
        pltpu.make_async_copy(v_ref, kv_buf.at[ROWS:], sem.at[1]),
        pltpu.make_async_copy(do_ref, out_ref.at[ROWS : 2 * ROWS], sem.at[2]),
        pltpu.make_async_copy(o_ref, o_buf, sem.at[3]),
        pltpu.make_async_copy(q_ref, out_ref.at[:ROWS], sem.at[4]),
    ]
    for copy in reads:
        copy.start()
    reads[0].wait()
    reads[1].wait()
    writes = [pltpu.make_async_copy(kv_buf, kv_ref.at[i], kv_sem.at[i]) for i in range(PEERS)]
    for copy in writes:
        copy.start()
    reads[2].wait()
    reads[3].wait()
    ones = jnp.ones((8, HEAD), jnp.float32)
    dots = []
    for b in range(2):
        at = slice(b * BLOCK, (b + 1) * BLOCK)
        at2 = slice(ROWS + b * BLOCK, ROWS + (b + 1) * BLOCK)
        prod = jnp.concatenate(
            [
                out_ref[at2, head(h)].astype(jnp.float32) * o_buf[at, head(h)].astype(jnp.float32)
                for h in range(HEADS)
            ],
            0,
        )
        dots.append(
            lax.dot_general(
                ones, prod, NT, precision=lax.Precision.HIGHEST, preferred_element_type=jnp.float32
            )[:1]
        )
    norms = terms_of(norm_ref[...])
    norms = jnp.concatenate(norms + [jnp.zeros((8, WIDTH - 3 * HEAD), jnp.float32)], 1)
    dots = terms_of(jnp.concatenate(dots, 1))
    dots = dots + [jnp.zeros((5, WIDTH), jnp.float32)]
    out_ref[2 * ROWS :] = jnp.concatenate([norms] + dots, 0).astype(jnp.bfloat16)
    reads[4].wait()
    for copy in writes:
        copy.wait()


def stage(
    p0_ref, p1_ref, p2_ref, p3_ref, qs_ref, norm_ref, dot_ref, buf_ref, q_ref, do_ref, sem
):
    copies = [
        pltpu.make_async_copy(p_ref, buf_ref.at[g], sem.at[g])
        for g, p_ref in enumerate((p0_ref, p1_ref, p2_ref, p3_ref))
    ]
    for copy in copies:
        copy.start()
    for g, copy in enumerate(copies):
        copy.wait()
        p_ref = buf_ref.at[g]
        more = p_ref[2 * ROWS :, :].astype(jnp.float32)
        norm = (more[:8, head(0)] + more[:8, head(1)] + more[:8, head(2)]) * LOG2E
        turned = pltpu.roll(norm, BLOCK, 1)
        left = lax.broadcasted_iota(jnp.int32, (1, HEAD), 1) < BLOCK
        dots = more[8:9] + more[9:10] + more[10:11]
        for i in range(2):
            b = 2 * g + i
            dot_ref[b : b + 1, :] = dots[:, i * LANES : (i + 1) * LANES]
            one, two = (norm, turned) if i == 0 else (turned, norm)
            for t in range(HEADS // 2):
                norm_ref[b : b + 1, t * HEAD : (t + 1) * HEAD] = jnp.where(
                    left, one[2 * t : 2 * t + 1], two[2 * t + 1 : 2 * t + 2]
                )
            for h in range(HEADS):
                to = slice(b * LANES + h * BLOCK, b * LANES + (h + 1) * BLOCK)
                q_ref[to, :] = p_ref[i * BLOCK : (i + 1) * BLOCK, head(h)]
                do_ref[to, :] = p_ref[ROWS + i * BLOCK : ROWS + (i + 1) * BLOCK, head(h)]
    copies = [
        pltpu.make_async_copy(q_ref, qs_ref.at[0], sem.at[0]),
        pltpu.make_async_copy(do_ref, qs_ref.at[1], sem.at[1]),
    ]
    for copy in copies:
        copy.start()
    for copy in copies:
        copy.wait()


def terms(
    work_ref, held_ref, place_ref, first_ref, own_ref, norm_ref, dot_ref, kv_ref, qs_ref,
    dqt_ref, dkv_ref, acc_ref, half_ref, q_ref, do_ref, sem,
):
    reads = [
        pltpu.make_async_copy(qs_ref.at[0], q_ref, sem.at[0]),
        pltpu.make_async_copy(qs_ref.at[1], do_ref, sem.at[1]),
    ]
    for copy in reads:
        copy.start()
    acc_ref[...] = jnp.zeros_like(acc_ref)
    dqt_ref[...] = jnp.zeros_like(dqt_ref)
    for copy in reads:
        copy.wait()

    def one(t):
        b, j = work_ref[t], work_ref[SLOTS + t]
        a0 = pl.multiple_of(place_ref[j], BLOCK)
        a1 = pl.multiple_of(place_ref[j + 1], BLOCK)
        rows = pl.ds(pl.multiple_of(b * LANES, LANES), LANES)
        q, do = q_ref[rows, :], do_ref[rows, :]
        k = jnp.concatenate([kv_ref[pl.ds(a0, BLOCK), :], kv_ref[pl.ds(a1, BLOCK), :]], 0)
        v = jnp.concatenate(
            [kv_ref[pl.ds(a0 + ROWS, BLOCK), :], kv_ref[pl.ds(a1 + ROWS, BLOCK), :]], 0
        )
        s = lax.dot_general(k, q, NT, preferred_element_type=jnp.float32)
        dp = lax.dot_general(v, do, NT, preferred_element_type=jnp.float32)
        lane = lax.broadcasted_iota(jnp.int32, (BLOCK, LANES), 0)
        pos = jnp.concatenate([lane + held_ref[j] * BLOCK, lane + held_ref[j + 1] * BLOCK], 0)
        at = pl.ds(b, 1)
        ok = (pos >= first_ref[at, :]) & (pos <= own_ref[at, :])
        w = jnp.where(ok, jnp.exp2(s * (SCALE * LOG2E) - norm_ref[at, :]), 0.0)
        ds = (w * (dp - dot_ref[at, :]) * SCALE).astype(jnp.bfloat16)
        dv = jnp.dot(w.astype(jnp.bfloat16), do, preferred_element_type=jnp.float32)
        dk = jnp.dot(ds, q, preferred_element_type=jnp.float32)
        dqt = lax.dot_general(k, ds, TN, preferred_element_type=jnp.float32)
        return b, a0, a1, dqt, dk, dv

    def two(i, carry):
        for b, a0, a1, dqt, dk, dv in [one(2 * i), one(2 * i + 1)]:
            dqt_ref[pl.ds(pl.multiple_of(b * HEAD, HEAD), HEAD), :] += dqt
            acc_ref[pl.ds(a0, BLOCK), :] += dk[:BLOCK]
            acc_ref[pl.ds(a1, BLOCK), :] += dk[BLOCK:]
            acc_ref[pl.ds(a0 + ROWS, BLOCK), :] += dv[:BLOCK]
            acc_ref[pl.ds(a1 + ROWS, BLOCK), :] += dv[BLOCK:]
        return carry

    lax.fori_loop(0, work_ref[2 * SLOTS], two, 0)
    copies = []
    for i in range(4):
        at = pl.ds(i * 2 * PEERS * BLOCK // 2, PEERS * BLOCK)
        half_ref[at, :] = acc_ref[at, :].astype(jnp.bfloat16)
        copies.append(pltpu.make_async_copy(half_ref.at[at], dkv_ref.at[at], sem.at[i]))
        copies[-1].start()
    for copy in copies:
        copy.wait()


def unstage(dqt_ref, dq0_ref, dq1_ref, dq2_ref, dq3_ref):
    for b in range(8):
        out = (dq0_ref, dq1_ref, dq2_ref, dq3_ref)[b // 2]
        at = slice((b % 2) * BLOCK, (b % 2 + 1) * BLOCK)
        dq = dqt_ref[b * HEAD : (b + 1) * HEAD, :].T.astype(out.dtype)
        for h in range(HEADS):
            out[at, head(h)] = dq[h * BLOCK : (h + 1) * BLOCK]


def total(got_ref, k_ref, v_ref):
    both = got_ref[0].astype(jnp.float32)
    for i in range(1, PEERS):
        both = both + got_ref[i].astype(jnp.float32)
    k_ref[...] = both[:ROWS].astype(jnp.bfloat16)
    v_ref[...] = both[ROWS:].astype(jnp.bfloat16)


def plan(doc_lengths, block_order, yh, xh, xl, core):
    docs, nblk = doc_lengths.shape[0], block_order.shape[0]
    nheld = nblk // 4
    upto = jnp.arange(docs)[:, None] >= jnp.arange(docs)[None, :]
    ends = jnp.sum(jnp.where(upto, doc_lengths[None, :], 0), axis=1)
    blocks = jnp.arange(nblk, dtype=jnp.int32)
    held_here = ((blocks // 2) % 2 == core) & ((blocks // 4) % 2 == xl)
    place = (blocks // 8) * (2 * ROWS) + (blocks % 2) * BLOCK
    before = held_here[None, :] & (block_order[None, :] < block_order[:, None])
    rank = jnp.sum(before.astype(jnp.int32), axis=1)
    slots = jnp.arange(nheld + 8, dtype=jnp.int32)
    hit = held_here[None, :] & (rank[None, :] == slots[:, None])
    held = jnp.sum(jnp.where(hit, block_order[None, :], 0), axis=1)
    held = jnp.where(slots < nheld, held, nblk)
    place = jnp.sum(jnp.where(hit, place[None, :], 0), axis=1)
    x, turn = 2 * xh + xl, 1 - 2 * core
    owners = 8 * yh + jnp.stack(
        [
            2 * x + core,
            2 * x + 1 - core,
            2 * ((x + turn) % 4) + core,
            2 * ((x - turn) % 4) + 1 - core,
        ]
    )
    stored = (2 * owners[:, None] + jnp.arange(2)[None, :]).reshape(8)
    mine = jnp.sum(jnp.where(stored[:, None] == blocks[None, :], block_order[None, :], 0), axis=1)
    pos = mine[:, None] * BLOCK + jnp.arange(BLOCK, dtype=jnp.int32)[None, :]
    first = jnp.max(jnp.where(ends[None, None, :] <= pos[:, :, None], ends[None, None, :], 0), axis=2)
    begin = jnp.sum((held[None, :] < (first[:, :1] >> 6)).astype(jnp.int32), axis=1)
    until = jnp.sum((held[None, :] <= mine[:, None]).astype(jnp.int32), axis=1)
    pairs = (until - begin + 1) >> 1
    eight = jnp.arange(8)
    stops = jnp.sum(jnp.where(eight[:, None] >= eight[None, :], pairs[None, :], 0), axis=1)
    place_in = jnp.arange(SLOTS, dtype=jnp.int32)
    done = stops[None, :] <= place_in[:, None]
    of = jnp.sum(done.astype(jnp.int32), axis=1)
    this = of[:, None] == eight[None, :]
    at = jnp.sum(jnp.where(this, begin[None, :] - 2 * (stops - pairs)[None, :], 0), axis=1)
    at = jnp.where(of < 8, at + 2 * place_in, nheld)
    work = jnp.concatenate([jnp.minimum(of, 7), at, (stops[-1:] + 1) >> 1])
    return work, held, place, jnp.tile(first, (1, HEADS)), jnp.tile(pos, (1, HEADS))


def on_device(queries, keys, values, attn_out, grad_out, log_norm, doc_lengths, block_order):
    f32, bf16 = jnp.float32, jnp.bfloat16
    shape = jax.ShapeDtypeStruct
    place = [lax.axis_index(a) for a in CTX]
    dma = pltpu.SemaphoreType.DMA

    swap = [(0, 1), (1, 0)]
    there = [(2 * ((i + 1) % 4), 2 * i) for i in range(4)]
    there += [(2 * i + 1, 2 * ((i + 1) % 4) + 1) for i in range(4)]
    back = [(j, i) for i, j in there]
    across = [(2 * i, 2 * ((i - 1) % 4) + 1) for i in range(4)]
    across += [(2 * i + 1, 2 * ((i + 1) % 4)) for i in range(4)]
    spread, p0 = call(
        pack,
        (pltpu.HBM((PEERS, 2 * ROWS, HEAD), bf16), shape((2 * ROWS + EXTRA, WIDTH), bf16)),
        [HBM] * 5 + [VMEM],
        (HBM, VMEM),
        *map(in_hbm, (keys, values, queries, grad_out, attn_out)), log_norm,
        scratch=[
            pltpu.VMEM((2 * ROWS, HEAD), bf16),
            pltpu.VMEM((ROWS, WIDTH), bf16),
            dma((5,)),
            dma((PEERS,)),
        ],
    )
    p2 = lax.ppermute(p0, NEXT, there)
    kv = lax.all_to_all(spread, KEEPERS, 0, 0, tiled=True)
    p1 = lax.ppermute(p0, "core", swap)
    p3 = lax.ppermute(p2, "core", swap)
    listed = plan(doc_lengths, block_order, *place)
    p3, (work, held, at, first, own) = lax.optimization_barrier((p3, listed))
    qs, norm, dot = call(
        stage,
        (pltpu.HBM((2, 8 * LANES, HEAD), bf16),) + (shape((8, LANES), f32),) * 2,
        [HBM] * 4,
        (HBM, VMEM, VMEM),
        *map(in_hbm, (p0, p1, p2, p3)),
        scratch=[
            pltpu.VMEM((4, 2 * ROWS + EXTRA, WIDTH), bf16),
            pltpu.VMEM((8 * LANES, HEAD), bf16),
            pltpu.VMEM((8 * LANES, HEAD), bf16),
            dma((4,)),
        ],
    )
    nkeys = 2 * PEERS * ROWS
    dqt, dkv = call(
        terms,
        (shape((8 * HEAD, LANES), f32), pltpu.HBM((nkeys, HEAD), bf16)),
        [SMEM] * 3 + [VMEM] * 5 + [HBM],
        (VMEM, HBM),
        work, held, at, first, own, norm, dot, kv.reshape(nkeys, HEAD), in_hbm(qs),
        scratch=[
            pltpu.VMEM((nkeys, HEAD), f32),
            pltpu.VMEM((nkeys, HEAD), bf16),
            pltpu.VMEM((8 * LANES, HEAD), bf16),
            pltpu.VMEM((8 * LANES, HEAD), bf16),
            dma((4,)),
        ],
    )
    got = lax.all_to_all(dkv.reshape(PEERS, 2 * ROWS, HEAD), KEEPERS, 0, 0, tiled=True)
    dq0, *others = call(
        unstage,
        (shape((ROWS, WIDTH), f32),) + (shape((ROWS, WIDTH), bf16),) * 3,
        [VMEM],
        (VMEM,) * 4,
        dqt,
    )
    routes = (("core", swap), (NEXT, back), (NEXT, across))
    parts = [lax.ppermute(x, axes, route) for x, (axes, route) in zip(others, routes)]
    grad_q = (dq0 + sum(x.astype(f32) for x in parts)).astype(bf16)
    grad_k, grad_v = call(total, (shape((ROWS, HEAD), bf16),) * 2, [VMEM], (VMEM,) * 2, got)
    return grad_q, grad_k, grad_v


def solution(mesh):
    parts = Mesh(
        mesh.devices.reshape(2, 4, 2, 2, 2, 8), ("dp", "yh", "xh", "xl", "core", "tensor")
    )
    seq = ("dp",) + CTX
    wide = P(seq, "tensor")
    return jax.shard_map(
        on_device,
        mesh=parts,
        in_specs=(wide,) * 5 + (P("tensor", seq), P("dp"), P("dp")),
        out_specs=(wide, wide, wide),
        check_vma=False,
    )
```

```python
import math

import jax
import jax.numpy as jnp
from jax import lax
from jax.experimental import pallas as pl
from jax.experimental.pallas import tpu as pltpu
from jax.sharding import Mesh
from jax.sharding import PartitionSpec as P

HEADS = 8
HEAD = 128
BLOCK = 64
ROWS = 2 * BLOCK
WIDTH = HEADS * HEAD
LANES = HEADS * BLOCK
EXTRA = 16
PEERS = 8
SLOTS = 72
SCALE = 1.0 / math.sqrt(HEAD)
LOG2E = math.log2(math.e)
CTX = ("yh", "xh", "xl", "core")
KEEPERS = ("yh", "xh")
NEXT = ("xh", "xl", "core")
NT = (((1,), (1,)), ((), ()))
TN = (((0,), (0,)), ((), ()))
VMEM = pl.BlockSpec(memory_space=pltpu.VMEM)
SMEM = pl.BlockSpec(memory_space=pltpu.SMEM)
HBM = pl.BlockSpec(memory_space=pltpu.HBM)


def head(h):
    return slice(h * HEAD, (h + 1) * HEAD)


def in_hbm(x):
    return pltpu.with_memory_space_constraint(x, pltpu.HBM)


def call(kernel, out, ins, outs, *args, scratch=(), limit=16):
    return pl.pallas_call(
        kernel,
        out_shape=out,
        in_specs=ins,
        out_specs=outs,
        scratch_shapes=scratch,
        compiler_params=pltpu.CompilerParams(vmem_limit_bytes=limit << 20),
        name=kernel.__name__,
    )(*args)


def terms_of(x):
    parts = []
    for _ in range(3):
        term = x.astype(jnp.bfloat16).astype(jnp.float32)
        parts.append(term)
        x = x - term
    return parts


def spread(k_ref, v_ref, kv_ref, kv_buf, sem, kv_sem):
    reads = [
        pltpu.make_async_copy(k_ref, kv_buf.at[:ROWS], sem.at[0]),
        pltpu.make_async_copy(v_ref, kv_buf.at[ROWS:], sem.at[1]),
    ]
    for copy in reads:
        copy.start()
    for copy in reads:
        copy.wait()
    writes = [pltpu.make_async_copy(kv_buf, kv_ref.at[i], kv_sem.at[i]) for i in range(PEERS)]
    for copy in writes:
        copy.start()
    for copy in writes:
        copy.wait()


def pack(q_ref, do_ref, o_ref, norm_ref, out_ref, o_buf, norm_buf, sem):
    reads = [
        pltpu.make_async_copy(do_ref, out_ref.at[ROWS : 2 * ROWS], sem.at[0]),
        pltpu.make_async_copy(o_ref, o_buf, sem.at[1]),
        pltpu.make_async_copy(norm_ref, norm_buf, sem.at[2]),
        pltpu.make_async_copy(q_ref, out_ref.at[:ROWS], sem.at[3]),
    ]
    for copy in reads:
        copy.start()
    for copy in reads[:3]:
        copy.wait()
    ones = jnp.ones((8, HEAD), jnp.float32)
    dots = []
    for b in range(2):
        at = slice(b * BLOCK, (b + 1) * BLOCK)
        at2 = slice(ROWS + b * BLOCK, ROWS + (b + 1) * BLOCK)
        prod = jnp.concatenate(
            [
                out_ref[at2, head(h)].astype(jnp.float32) * o_buf[at, head(h)].astype(jnp.float32)
                for h in range(HEADS)
            ],
            0,
        )
        dots.append(
            lax.dot_general(
                ones, prod, NT, precision=lax.Precision.HIGHEST, preferred_element_type=jnp.float32
            )[:1]
        )
    norms = terms_of(norm_buf[...])
    norms = jnp.concatenate(norms + [jnp.zeros((8, WIDTH - 3 * HEAD), jnp.float32)], 1)
    dots = terms_of(jnp.concatenate(dots, 1))
    dots = dots + [jnp.zeros((5, WIDTH), jnp.float32)]
    out_ref[2 * ROWS :] = jnp.concatenate([norms] + dots, 0).astype(jnp.bfloat16)
    reads[3].wait()


def stage(p_refs, q_ref, do_ref, norm_ref, dot_ref):
    for g, p_ref in enumerate(p_refs):
        more = p_ref[2 * ROWS :, :].astype(jnp.float32)
        norm = (more[:8, head(0)] + more[:8, head(1)] + more[:8, head(2)]) * LOG2E
        turned = pltpu.roll(norm, BLOCK, 1)
        left = lax.broadcasted_iota(jnp.int32, (1, HEAD), 1) < BLOCK
        dots = more[8:9] + more[9:10] + more[10:11]
        for i in range(2):
            b = 2 * g + i
            dot_ref[b : b + 1, :] = dots[:, i * LANES : (i + 1) * LANES]
            one, two = (norm, turned) if i == 0 else (turned, norm)
            for t in range(HEADS // 2):
                norm_ref[b : b + 1, t * HEAD : (t + 1) * HEAD] = jnp.where(
                    left, one[2 * t : 2 * t + 1], two[2 * t + 1 : 2 * t + 2]
                )
            for h in range(HEADS):
                to = slice(b * LANES + h * BLOCK, b * LANES + (h + 1) * BLOCK)
                q_ref[to, :] = p_ref[i * BLOCK : (i + 1) * BLOCK, head(h)]
                do_ref[to, :] = p_ref[ROWS + i * BLOCK : ROWS + (i + 1) * BLOCK, head(h)]


def terms(
    work_ref, held_ref, place_ref, first_ref, own_ref, p0_ref, p1_ref, p2_ref, p3_ref, kv_ref,
    dqs_ref, dkv_ref, acc_ref, half_ref, dqt_ref, q_ref, do_ref, norm_ref, dot_ref, sem,
):
    acc_ref[...] = jnp.zeros_like(acc_ref)
    dqt_ref[...] = jnp.zeros_like(dqt_ref)
    stage((p0_ref, p1_ref, p2_ref, p3_ref), q_ref, do_ref, norm_ref, dot_ref)

    def one(t):
        b, j = work_ref[t], work_ref[SLOTS + t]
        a0 = pl.multiple_of(place_ref[j], BLOCK)
        a1 = pl.multiple_of(place_ref[j + 1], BLOCK)
        rows = pl.ds(pl.multiple_of(b * LANES, LANES), LANES)
        q, do = q_ref[rows, :], do_ref[rows, :]
        k = jnp.concatenate([kv_ref[pl.ds(a0, BLOCK), :], kv_ref[pl.ds(a1, BLOCK), :]], 0)
        v = jnp.concatenate(
            [kv_ref[pl.ds(a0 + ROWS, BLOCK), :], kv_ref[pl.ds(a1 + ROWS, BLOCK), :]], 0
        )
        s = lax.dot_general(k, q, NT, preferred_element_type=jnp.float32)
        dp = lax.dot_general(v, do, NT, preferred_element_type=jnp.float32)
        lane = lax.broadcasted_iota(jnp.int32, (BLOCK, LANES), 0)
        pos = jnp.concatenate([lane + held_ref[j] * BLOCK, lane + held_ref[j + 1] * BLOCK], 0)
        at = pl.ds(b, 1)
        ok = (pos >= first_ref[at, :]) & (pos <= own_ref[at, :])
        w = jnp.where(ok, jnp.exp2(s * (SCALE * LOG2E) - norm_ref[at, :]), 0.0)
        ds = (w * (dp - dot_ref[at, :]) * SCALE).astype(jnp.bfloat16)
        dv = jnp.dot(w.astype(jnp.bfloat16), do, preferred_element_type=jnp.float32)
        dk = jnp.dot(ds, q, preferred_element_type=jnp.float32)
        dqt = lax.dot_general(k, ds, TN, preferred_element_type=jnp.float32)
        return b, a0, a1, dqt, dk, dv

    def two(i, carry):
        for b, a0, a1, dqt, dk, dv in [one(2 * i), one(2 * i + 1)]:
            dqt_ref[pl.ds(pl.multiple_of(b * HEAD, HEAD), HEAD), :] += dqt
            acc_ref[pl.ds(a0, BLOCK), :] += dk[:BLOCK]
            acc_ref[pl.ds(a1, BLOCK), :] += dk[BLOCK:]
            acc_ref[pl.ds(a0 + ROWS, BLOCK), :] += dv[:BLOCK]
            acc_ref[pl.ds(a1 + ROWS, BLOCK), :] += dv[BLOCK:]
        return carry

    lax.fori_loop(0, work_ref[2 * SLOTS], two, 0)
    copies = [pltpu.make_async_copy(dqt_ref, dqs_ref, sem.at[4])]
    copies[0].start()
    for i in range(4):
        at = pl.ds(i * 2 * PEERS * BLOCK // 2, PEERS * BLOCK)
        half_ref[at, :] = acc_ref[at, :].astype(jnp.bfloat16)
        copies.append(pltpu.make_async_copy(half_ref.at[at], dkv_ref.at[at], sem.at[i]))
        copies[-1].start()
    for copy in copies:
        copy.wait()


def unstage(dqs_ref, dq0_ref, dq1_ref, dq2_ref, dq3_ref, dqt_ref, sem):
    copies = []
    for b in (2, 3, 4, 5, 6, 7, 0, 1):
        at = slice(b * HEAD, (b + 1) * HEAD)
        copies.append(pltpu.make_async_copy(dqs_ref.at[at], dqt_ref.at[at], sem.at[b]))
        copies[-1].start()
    for copy in copies:
        copy.wait()
    for b in range(8):
        out = (dq0_ref, dq1_ref, dq2_ref, dq3_ref)[b // 2]
        at = slice((b % 2) * BLOCK, (b % 2 + 1) * BLOCK)
        dq = dqt_ref[b * HEAD : (b + 1) * HEAD, :].T.astype(out.dtype)
        for h in range(HEADS):
            out[at, head(h)] = dq[h * BLOCK : (h + 1) * BLOCK]


def total(got_ref, k_ref, v_ref):
    both = got_ref[0].astype(jnp.float32)
    for i in range(1, PEERS):
        both = both + got_ref[i].astype(jnp.float32)
    k_ref[...] = both[:ROWS].astype(jnp.bfloat16)
    v_ref[...] = both[ROWS:].astype(jnp.bfloat16)


def plan(doc_lengths, block_order, yh, xh, xl, core):
    docs, nblk = doc_lengths.shape[0], block_order.shape[0]
    nheld = nblk // 4
    upto = jnp.arange(docs)[:, None] >= jnp.arange(docs)[None, :]
    ends = jnp.sum(jnp.where(upto, doc_lengths[None, :], 0), axis=1)
    blocks = jnp.arange(nblk, dtype=jnp.int32)
    held_here = ((blocks // 2) % 2 == core) & ((blocks // 4) % 2 == xl)
    place = (blocks // 8) * (2 * ROWS) + (blocks % 2) * BLOCK
    before = held_here[None, :] & (block_order[None, :] < block_order[:, None])
    rank = jnp.sum(before.astype(jnp.int32), axis=1)
    slots = jnp.arange(nheld + 8, dtype=jnp.int32)
    hit = held_here[None, :] & (rank[None, :] == slots[:, None])
    held = jnp.sum(jnp.where(hit, block_order[None, :], 0), axis=1)
    held = jnp.where(slots < nheld, held, nblk)
    place = jnp.sum(jnp.where(hit, place[None, :], 0), axis=1)
    x, turn = 2 * xh + xl, 1 - 2 * core
    owners = 8 * yh + jnp.stack(
        [
            2 * x + core,
            2 * x + 1 - core,
            2 * ((x + turn) % 4) + core,
            2 * ((x - turn) % 4) + 1 - core,
        ]
    )
    stored = (2 * owners[:, None] + jnp.arange(2)[None, :]).reshape(8)
    mine = jnp.sum(jnp.where(stored[:, None] == blocks[None, :], block_order[None, :], 0), axis=1)
    pos = mine[:, None] * BLOCK + jnp.arange(BLOCK, dtype=jnp.int32)[None, :]
    first = jnp.max(jnp.where(ends[None, None, :] <= pos[:, :, None], ends[None, None, :], 0), axis=2)
    begin = jnp.sum((held[None, :] < (first[:, :1] >> 6)).astype(jnp.int32), axis=1)
    until = jnp.sum((held[None, :] <= mine[:, None]).astype(jnp.int32), axis=1)
    pairs = (until - begin + 1) >> 1
    eight = jnp.arange(8)
    stops = jnp.sum(jnp.where(eight[:, None] >= eight[None, :], pairs[None, :], 0), axis=1)
    place_in = jnp.arange(SLOTS, dtype=jnp.int32)
    done = stops[None, :] <= place_in[:, None]
    of = jnp.sum(done.astype(jnp.int32), axis=1)
    this = of[:, None] == eight[None, :]
    at = jnp.sum(jnp.where(this, begin[None, :] - 2 * (stops - pairs)[None, :], 0), axis=1)
    at = jnp.where(of < 8, at + 2 * place_in, nheld)
    work = jnp.concatenate([jnp.minimum(of, 7), at, (stops[-1:] + 1) >> 1])
    return work, held, place, jnp.tile(first, (1, HEADS)), jnp.tile(pos, (1, HEADS))


def on_device(queries, keys, values, attn_out, grad_out, log_norm, doc_lengths, block_order):
    f32, bf16 = jnp.float32, jnp.bfloat16
    shape = jax.ShapeDtypeStruct
    place = [lax.axis_index(a) for a in CTX]
    dma = pltpu.SemaphoreType.DMA

    swap = [(0, 1), (1, 0)]
    there = [(2 * ((i + 1) % 4), 2 * i) for i in range(4)]
    there += [(2 * i + 1, 2 * ((i + 1) % 4) + 1) for i in range(4)]
    back = [(j, i) for i, j in there]
    across = [(2 * i, 2 * ((i - 1) % 4) + 1) for i in range(4)]
    across += [(2 * i + 1, 2 * ((i + 1) % 4)) for i in range(4)]
    sent = call(
        spread,
        pltpu.HBM((PEERS, 2 * ROWS, HEAD), bf16),
        [HBM] * 2,
        HBM,
        in_hbm(keys), in_hbm(values),
        scratch=[pltpu.VMEM((2 * ROWS, HEAD), bf16), dma((2,)), dma((PEERS,))],
    )
    kv = lax.all_to_all(sent, KEEPERS, 0, 0, tiled=True)
    p0 = call(
        pack,
        shape((2 * ROWS + EXTRA, WIDTH), bf16),
        [HBM] * 4,
        VMEM,
        *map(in_hbm, (queries, grad_out, attn_out, log_norm)),
        scratch=[pltpu.VMEM((ROWS, WIDTH), bf16), pltpu.VMEM((HEADS, ROWS), f32), dma((4,))],
    )
    p2 = lax.ppermute(p0, NEXT, there)
    p3 = lax.ppermute(p2, "core", swap)
    p1 = lax.ppermute(lax.optimization_barrier((p0, p2))[0], "core", swap)
    work, held, at, first, own = plan(doc_lengths, block_order, *place)
    nkeys = 2 * PEERS * ROWS
    dqs, dkv = call(
        terms,
        (pltpu.HBM((8 * HEAD, LANES), f32), pltpu.HBM((nkeys, HEAD), bf16)),
        [SMEM] * 3 + [VMEM] * 7,
        (HBM, HBM),
        work, held, at, first, own, p0, p1, p2, p3, kv.reshape(nkeys, HEAD),
        scratch=[
            pltpu.VMEM((nkeys, HEAD), f32),
            pltpu.VMEM((nkeys, HEAD), bf16),
            pltpu.VMEM((8 * HEAD, LANES), f32),
            pltpu.VMEM((8 * LANES, HEAD), bf16),
            pltpu.VMEM((8 * LANES, HEAD), bf16),
            pltpu.VMEM((8, LANES), f32),
            pltpu.VMEM((8, LANES), f32),
            dma((5,)),
        ],
    )
    got = lax.all_to_all(dkv.reshape(PEERS, 2 * ROWS, HEAD), KEEPERS, 0, 0, tiled=True)
    dq0, *others = call(
        unstage,
        (shape((ROWS, WIDTH), f32),) + (shape((ROWS, WIDTH), bf16),) * 3,
        [HBM],
        (VMEM,) * 4,
        in_hbm(dqs),
        scratch=[pltpu.VMEM((8 * HEAD, LANES), f32), dma((8,))],
    )
    routes = (("core", swap), (NEXT, back), (NEXT, across))
    parts = [lax.ppermute(x, axes, route) for x, (axes, route) in zip(others, routes)]
    grad_q = (dq0 + sum(x.astype(f32) for x in parts)).astype(bf16)
    grad_k, grad_v = call(total, (shape((ROWS, HEAD), bf16),) * 2, [VMEM], (VMEM,) * 2, got)
    return grad_q, grad_k, grad_v


def solution(mesh):
    parts = Mesh(
        mesh.devices.reshape(2, 4, 2, 2, 2, 8), ("dp", "yh", "xh", "xl", "core", "tensor")
    )
    seq = ("dp",) + CTX
    wide = P(seq, "tensor")
    return jax.shard_map(
        on_device,
        mesh=parts,
        in_specs=(wide,) * 5 + (P("tensor", seq), P("dp"), P("dp")),
        out_specs=(wide, wide, wide),
        check_vma=False,
    )
```

```python
import math

import jax
import jax.numpy as jnp
from jax import lax
from jax.experimental import pallas as pl
from jax.experimental.pallas import tpu as pltpu
from jax.sharding import Mesh
from jax.sharding import PartitionSpec as P

HEADS = 8
HEAD = 128
BLOCK = 64
ROWS = 2 * BLOCK
WIDTH = HEADS * HEAD
LANES = HEADS * BLOCK
EXTRA = 16
PEERS = 8
SLOTS = 72
SCALE = 1.0 / math.sqrt(HEAD)
LOG2E = math.log2(math.e)
CTX = ("yh", "xh", "xl", "core")
KEEPERS = ("yh", "xh")
NEXT = ("xh", "xl", "core")
NT = (((1,), (1,)), ((), ()))
TN = (((0,), (0,)), ((), ()))
VMEM = pl.BlockSpec(memory_space=pltpu.VMEM)
SMEM = pl.BlockSpec(memory_space=pltpu.SMEM)
HBM = pl.BlockSpec(memory_space=pltpu.HBM)


def head(h):
    return slice(h * HEAD, (h + 1) * HEAD)


def in_hbm(x):
    return pltpu.with_memory_space_constraint(x, pltpu.HBM)


def call(kernel, out, ins, outs, *args, scratch=(), limit=16):
    return pl.pallas_call(
        kernel,
        out_shape=out,
        in_specs=ins,
        out_specs=outs,
        scratch_shapes=scratch,
        compiler_params=pltpu.CompilerParams(vmem_limit_bytes=limit << 20),
        name=kernel.__name__,
    )(*args)


def terms_of(x):
    parts = []
    for _ in range(3):
        term = x.astype(jnp.bfloat16).astype(jnp.float32)
        parts.append(term)
        x = x - term
    return parts


def pack(
    k_ref, v_ref, q_ref, do_ref, o_ref, norm_ref,
    kv_ref, out_ref, kv_buf, o_buf, norm_buf, sem, kv_sem,
):
    reads = [
        pltpu.make_async_copy(k_ref, kv_buf.at[:ROWS], sem.at[0]),
        pltpu.make_async_copy(v_ref, kv_buf.at[ROWS:], sem.at[1]),
        pltpu.make_async_copy(do_ref, out_ref.at[ROWS : 2 * ROWS], sem.at[2]),
        pltpu.make_async_copy(o_ref, o_buf, sem.at[3]),
        pltpu.make_async_copy(norm_ref, norm_buf, sem.at[4]),
        pltpu.make_async_copy(q_ref, out_ref.at[:ROWS], sem.at[5]),
    ]
    for copy in reads:
        copy.start()
    for copy in reads[:2]:
        copy.wait()
    writes = [pltpu.make_async_copy(kv_buf, kv_ref.at[i], kv_sem.at[i]) for i in range(PEERS)]
    for copy in writes:
        copy.start()
    for copy in reads[2:5]:
        copy.wait()
    ones = jnp.ones((8, HEAD), jnp.float32)
    dots = []
    for b in range(2):
        at = slice(b * BLOCK, (b + 1) * BLOCK)
        at2 = slice(ROWS + b * BLOCK, ROWS + (b + 1) * BLOCK)
        prod = jnp.concatenate(
            [
                out_ref[at2, head(h)].astype(jnp.float32) * o_buf[at, head(h)].astype(jnp.float32)
                for h in range(HEADS)
            ],
            0,
        )
        dots.append(
            lax.dot_general(
                ones, prod, NT, precision=lax.Precision.HIGHEST, preferred_element_type=jnp.float32
            )[:1]
        )
    norms = terms_of(norm_buf[...])
    norms = jnp.concatenate(norms + [jnp.zeros((8, WIDTH - 3 * HEAD), jnp.float32)], 1)
    dots = terms_of(jnp.concatenate(dots, 1))
    dots = dots + [jnp.zeros((5, WIDTH), jnp.float32)]
    out_ref[2 * ROWS :] = jnp.concatenate([norms] + dots, 0).astype(jnp.bfloat16)
    reads[5].wait()
    for copy in writes:
        copy.wait()


def stage(p_refs, q_ref, do_ref, norm_ref, dot_ref):
    for g, p_ref in enumerate(p_refs):
        more = p_ref[2 * ROWS :, :].astype(jnp.float32)
        norm = (more[:8, head(0)] + more[:8, head(1)] + more[:8, head(2)]) * LOG2E
        turned = pltpu.roll(norm, BLOCK, 1)
        left = lax.broadcasted_iota(jnp.int32, (1, HEAD), 1) < BLOCK
        dots = more[8:9] + more[9:10] + more[10:11]
        for i in range(2):
            b = 2 * g + i
            dot_ref[b : b + 1, :] = dots[:, i * LANES : (i + 1) * LANES]
            one, two = (norm, turned) if i == 0 else (turned, norm)
            for t in range(HEADS // 2):
                norm_ref[b : b + 1, t * HEAD : (t + 1) * HEAD] = jnp.where(
                    left, one[2 * t : 2 * t + 1], two[2 * t + 1 : 2 * t + 2]
                )
            for h in range(HEADS):
                to = slice(b * LANES + h * BLOCK, b * LANES + (h + 1) * BLOCK)
                q_ref[to, :] = p_ref[i * BLOCK : (i + 1) * BLOCK, head(h)]
                do_ref[to, :] = p_ref[ROWS + i * BLOCK : ROWS + (i + 1) * BLOCK, head(h)]


def terms(
    work_ref, held_ref, place_ref, first_ref, own_ref, p0_ref, p1_ref, p2_ref, p3_ref, kv_ref,
    dq0_ref, dq1_ref, dq2_ref, dq3_ref, dkv_ref,
    acc_ref, half_ref, dqt_ref, own_buf, send_buf, q_ref, do_ref, norm_ref, dot_ref, sem,
):
    acc_ref[...] = jnp.zeros_like(acc_ref)
    dqt_ref[...] = jnp.zeros_like(dqt_ref)
    stage((p0_ref, p1_ref, p2_ref, p3_ref), q_ref, do_ref, norm_ref, dot_ref)

    def one(t):
        b, j = work_ref[t], work_ref[SLOTS + t]
        a0 = pl.multiple_of(place_ref[j], BLOCK)
        a1 = pl.multiple_of(place_ref[j + 1], BLOCK)
        rows = pl.ds(pl.multiple_of(b * LANES, LANES), LANES)
        q, do = q_ref[rows, :], do_ref[rows, :]
        k = jnp.concatenate([kv_ref[pl.ds(a0, BLOCK), :], kv_ref[pl.ds(a1, BLOCK), :]], 0)
        v = jnp.concatenate(
            [kv_ref[pl.ds(a0 + ROWS, BLOCK), :], kv_ref[pl.ds(a1 + ROWS, BLOCK), :]], 0
        )
        s = lax.dot_general(k, q, NT, preferred_element_type=jnp.float32)
        dp = lax.dot_general(v, do, NT, preferred_element_type=jnp.float32)
        lane = lax.broadcasted_iota(jnp.int32, (BLOCK, LANES), 0)
        pos = jnp.concatenate([lane + held_ref[j] * BLOCK, lane + held_ref[j + 1] * BLOCK], 0)
        at = pl.ds(b, 1)
        ok = (pos >= first_ref[at, :]) & (pos <= own_ref[at, :])
        w = jnp.where(ok, jnp.exp2(s * (SCALE * LOG2E) - norm_ref[at, :]), 0.0)
        ds = (w * (dp - dot_ref[at, :]) * SCALE).astype(jnp.bfloat16)
        dv = jnp.dot(w.astype(jnp.bfloat16), do, preferred_element_type=jnp.float32)
        dk = jnp.dot(ds, q, preferred_element_type=jnp.float32)
        dqt = lax.dot_general(k, ds, TN, preferred_element_type=jnp.float32)
        return b, a0, a1, dqt, dk, dv

    def two(i, carry):
        for b, a0, a1, dqt, dk, dv in [one(2 * i), one(2 * i + 1)]:
            dqt_ref[pl.ds(pl.multiple_of(b * HEAD, HEAD), HEAD), :] += dqt
            acc_ref[pl.ds(a0, BLOCK), :] += dk[:BLOCK]
            acc_ref[pl.ds(a1, BLOCK), :] += dk[BLOCK:]
            acc_ref[pl.ds(a0 + ROWS, BLOCK), :] += dv[:BLOCK]
            acc_ref[pl.ds(a1 + ROWS, BLOCK), :] += dv[BLOCK:]
        return carry

    lax.fori_loop(0, work_ref[2 * SLOTS], two, 0)
    copies = []
    for i in range(4):
        at = pl.ds(i * PEERS * BLOCK, PEERS * BLOCK)
        half_ref[at, :] = acc_ref[at, :].astype(jnp.bfloat16)
        copies.append(pltpu.make_async_copy(half_ref.at[at], dkv_ref.at[at], sem.at[i]))
        copies[-1].start()
    for g in (3, 2, 1, 0):
        out = send_buf.at[g - 1] if g else own_buf
        for i in range(2):
            b = 2 * g + i
            dq = dqt_ref[b * HEAD : (b + 1) * HEAD, :].T.astype(out.dtype)
            for h in range(HEADS):
                out[i * BLOCK : (i + 1) * BLOCK, head(h)] = dq[h * BLOCK : (h + 1) * BLOCK]
        to = (dq0_ref, dq1_ref, dq2_ref, dq3_ref)[g]
        copies.append(pltpu.make_async_copy(out, to, sem.at[4 + g]))
        copies[-1].start()
    for copy in copies:
        copy.wait()


def total(got_ref, k_ref, v_ref):
    both = got_ref[0].astype(jnp.float32)
    for i in range(1, PEERS):
        both = both + got_ref[i].astype(jnp.float32)
    k_ref[...] = both[:ROWS].astype(jnp.bfloat16)
    v_ref[...] = both[ROWS:].astype(jnp.bfloat16)


def plan(doc_lengths, block_order, yh, xh, xl, core):
    docs, nblk = doc_lengths.shape[0], block_order.shape[0]
    nheld = nblk // 4
    upto = jnp.arange(docs)[:, None] >= jnp.arange(docs)[None, :]
    ends = jnp.sum(jnp.where(upto, doc_lengths[None, :], 0), axis=1)
    blocks = jnp.arange(nblk, dtype=jnp.int32)
    held_here = ((blocks // 2) % 2 == core) & ((blocks // 4) % 2 == xl)
    place = (blocks // 8) * (2 * ROWS) + (blocks % 2) * BLOCK
    before = held_here[None, :] & (block_order[None, :] < block_order[:, None])
    rank = jnp.sum(before.astype(jnp.int32), axis=1)
    slots = jnp.arange(nheld + 8, dtype=jnp.int32)
    hit = held_here[None, :] & (rank[None, :] == slots[:, None])
    held = jnp.sum(jnp.where(hit, block_order[None, :], 0), axis=1)
    held = jnp.where(slots < nheld, held, nblk)
    place = jnp.sum(jnp.where(hit, place[None, :], 0), axis=1)
    x, turn = 2 * xh + xl, 1 - 2 * core
    owners = 8 * yh + jnp.stack(
        [
            2 * x + core,
            2 * x + 1 - core,
            2 * ((x + turn) % 4) + core,
            2 * ((x - turn) % 4) + 1 - core,
        ]
    )
    stored = (2 * owners[:, None] + jnp.arange(2)[None, :]).reshape(8)
    mine = jnp.sum(jnp.where(stored[:, None] == blocks[None, :], block_order[None, :], 0), axis=1)
    pos = mine[:, None] * BLOCK + jnp.arange(BLOCK, dtype=jnp.int32)[None, :]
    first = jnp.max(jnp.where(ends[None, None, :] <= pos[:, :, None], ends[None, None, :], 0), axis=2)
    begin = jnp.sum((held[None, :] < (first[:, :1] >> 6)).astype(jnp.int32), axis=1)
    until = jnp.sum((held[None, :] <= mine[:, None]).astype(jnp.int32), axis=1)
    pairs = (until - begin + 1) >> 1
    eight = jnp.arange(8)
    stops = jnp.sum(jnp.where(eight[:, None] >= eight[None, :], pairs[None, :], 0), axis=1)
    place_in = jnp.arange(SLOTS, dtype=jnp.int32)
    done = stops[None, :] <= place_in[:, None]
    of = jnp.sum(done.astype(jnp.int32), axis=1)
    this = of[:, None] == eight[None, :]
    at = jnp.sum(jnp.where(this, begin[None, :] - 2 * (stops - pairs)[None, :], 0), axis=1)
    at = jnp.where(of < 8, at + 2 * place_in, nheld)
    work = jnp.concatenate([jnp.minimum(of, 7), at, (stops[-1:] + 1) >> 1])
    return work, held, place, jnp.tile(first, (1, HEADS)), jnp.tile(pos, (1, HEADS))


def on_device(queries, keys, values, attn_out, grad_out, log_norm, doc_lengths, block_order):
    f32, bf16 = jnp.float32, jnp.bfloat16
    shape = jax.ShapeDtypeStruct
    place = [lax.axis_index(a) for a in CTX]
    dma = pltpu.SemaphoreType.DMA

    swap = [(0, 1), (1, 0)]
    there = [(2 * ((i + 1) % 4), 2 * i) for i in range(4)]
    there += [(2 * i + 1, 2 * ((i + 1) % 4) + 1) for i in range(4)]
    back = [(j, i) for i, j in there]
    across = [(2 * i, 2 * ((i - 1) % 4) + 1) for i in range(4)]
    across += [(2 * i + 1, 2 * ((i + 1) % 4)) for i in range(4)]
    sent, p0 = call(
        pack,
        (pltpu.HBM((PEERS, 2 * ROWS, HEAD), bf16), shape((2 * ROWS + EXTRA, WIDTH), bf16)),
        [HBM] * 6,
        (HBM, VMEM),
        *map(in_hbm, (keys, values, queries, grad_out, attn_out, log_norm)),
        scratch=[
            pltpu.VMEM((2 * ROWS, HEAD), bf16),
            pltpu.VMEM((ROWS, WIDTH), bf16),
            pltpu.VMEM((HEADS, ROWS), f32),
            dma((6,)),
            dma((PEERS,)),
        ],
    )
    kv = lax.all_to_all(sent, KEEPERS, 0, 0, tiled=True)
    p2 = lax.ppermute(p0, NEXT, there)
    p3 = lax.ppermute(p2, "core", swap)
    p1 = lax.ppermute(p0, "core", swap)
    work, held, at, first, own = plan(doc_lengths, block_order, *place)
    nkeys = 2 * PEERS * ROWS
    dq0, *others, dkv = call(
        terms,
        (pltpu.HBM((ROWS, WIDTH), f32),)
        + (pltpu.HBM((ROWS, WIDTH), bf16),) * 3
        + (pltpu.HBM((nkeys, HEAD), bf16),),
        [SMEM] * 3 + [VMEM] * 7,
        (HBM,) * 5,
        work, held, at, first, own, p0, p1, p2, p3, kv.reshape(nkeys, HEAD),
        scratch=[
            pltpu.VMEM((nkeys, HEAD), f32),
            pltpu.VMEM((nkeys, HEAD), bf16),
            pltpu.VMEM((8 * HEAD, LANES), f32),
            pltpu.VMEM((ROWS, WIDTH), f32),
            pltpu.VMEM((3, ROWS, WIDTH), bf16),
            pltpu.VMEM((8 * LANES, HEAD), bf16),
            pltpu.VMEM((8 * LANES, HEAD), bf16),
            pltpu.VMEM((8, LANES), f32),
            pltpu.VMEM((8, LANES), f32),
            dma((8,)),
        ],
    )
    got = lax.all_to_all(dkv.reshape(PEERS, 2 * ROWS, HEAD), KEEPERS, 0, 0, tiled=True)
    routes = (("core", swap), (NEXT, back), (NEXT, across))
    parts = [lax.ppermute(x, axes, route) for x, (axes, route) in zip(others, routes)]
    grad_q = (dq0 + sum(x.astype(f32) for x in parts)).astype(bf16)
    grad_k, grad_v = call(total, (shape((ROWS, HEAD), bf16),) * 2, [VMEM], (VMEM,) * 2, got)
    return grad_q, grad_k, grad_v


def solution(mesh):
    parts = Mesh(
        mesh.devices.reshape(2, 4, 2, 2, 2, 8), ("dp", "yh", "xh", "xl", "core", "tensor")
    )
    seq = ("dp",) + CTX
    wide = P(seq, "tensor")
    return jax.shard_map(
        on_device,
        mesh=parts,
        in_specs=(wide,) * 5 + (P("tensor", seq), P("dp"), P("dp")),
        out_specs=(wide, wide, wide),
        check_vma=False,
    )
```

```python
import math

import jax
import jax.numpy as jnp
from jax import lax
from jax.experimental import pallas as pl
from jax.experimental.pallas import tpu as pltpu
from jax.sharding import Mesh
from jax.sharding import PartitionSpec as P

HEADS = 8
HEAD = 128
BLOCK = 64
ROWS = 2 * BLOCK
WIDTH = HEADS * HEAD
LANES = HEADS * BLOCK
EXTRA = 16
PEERS = 8
SLOTS = 72
SCALE = 1.0 / math.sqrt(HEAD)
LOG2E = math.log2(math.e)
CTX = ("yh", "xh", "xl", "core")
KEEPERS = ("yh", "xh")
NEXT = ("xh", "xl", "core")
NT = (((1,), (1,)), ((), ()))
TN = (((0,), (0,)), ((), ()))
VMEM = pl.BlockSpec(memory_space=pltpu.VMEM)
SMEM = pl.BlockSpec(memory_space=pltpu.SMEM)
HBM = pl.BlockSpec(memory_space=pltpu.HBM)


def head(h):
    return slice(h * HEAD, (h + 1) * HEAD)


def in_hbm(x):
    return pltpu.with_memory_space_constraint(x, pltpu.HBM)


def call(kernel, out, ins, outs, *args, scratch=(), limit=16):
    return pl.pallas_call(
        kernel,
        out_shape=out,
        in_specs=ins,
        out_specs=outs,
        scratch_shapes=scratch,
        compiler_params=pltpu.CompilerParams(vmem_limit_bytes=limit << 20),
        name=kernel.__name__,
    )(*args)


def terms_of(x):
    parts = []
    for _ in range(3):
        term = x.astype(jnp.bfloat16).astype(jnp.float32)
        parts.append(term)
        x = x - term
    return parts


def pack(
    k_ref, v_ref, q_ref, do_ref, o_ref, norm_ref,
    kv_ref, out_ref, kv_buf, o_buf, norm_buf, sem, kv_sem,
):
    reads = [
        pltpu.make_async_copy(k_ref, kv_buf.at[:ROWS], sem.at[0]),
        pltpu.make_async_copy(v_ref, kv_buf.at[ROWS:], sem.at[1]),
        pltpu.make_async_copy(do_ref, out_ref.at[ROWS : 2 * ROWS], sem.at[2]),
        pltpu.make_async_copy(o_ref, o_buf, sem.at[3]),
        pltpu.make_async_copy(norm_ref, norm_buf, sem.at[4]),
        pltpu.make_async_copy(q_ref, out_ref.at[:ROWS], sem.at[5]),
    ]
    for copy in reads:
        copy.start()
    for copy in reads[:2]:
        copy.wait()
    writes = [pltpu.make_async_copy(kv_buf, kv_ref.at[i], kv_sem.at[i]) for i in range(PEERS)]
    for copy in writes:
        copy.start()
    for copy in reads[2:5]:
        copy.wait()
    ones = jnp.ones((8, HEAD), jnp.float32)
    dots = []
    for b in range(2):
        at = slice(b * BLOCK, (b + 1) * BLOCK)
        at2 = slice(ROWS + b * BLOCK, ROWS + (b + 1) * BLOCK)
        prod = jnp.concatenate(
            [
                out_ref[at2, head(h)].astype(jnp.float32) * o_buf[at, head(h)].astype(jnp.float32)
                for h in range(HEADS)
            ],
            0,
        )
        dots.append(
            lax.dot_general(
                ones, prod, NT, precision=lax.Precision.HIGHEST, preferred_element_type=jnp.float32
            )[:1]
        )
    norms = terms_of(norm_buf[...])
    norms = jnp.concatenate(norms + [jnp.zeros((8, WIDTH - 3 * HEAD), jnp.float32)], 1)
    dots = terms_of(jnp.concatenate(dots, 1))
    dots = dots + [jnp.zeros((5, WIDTH), jnp.float32)]
    out_ref[2 * ROWS :] = jnp.concatenate([norms] + dots, 0).astype(jnp.bfloat16)
    reads[5].wait()
    for copy in writes:
        copy.wait()


def stage(p_refs, q_ref, do_ref, norm_ref, dot_ref):
    for g, p_ref in enumerate(p_refs):
        more = p_ref[2 * ROWS :, :].astype(jnp.float32)
        norm = (more[:8, head(0)] + more[:8, head(1)] + more[:8, head(2)]) * LOG2E
        turned = pltpu.roll(norm, BLOCK, 1)
        left = lax.broadcasted_iota(jnp.int32, (1, HEAD), 1) < BLOCK
        dots = more[8:9] + more[9:10] + more[10:11]
        for i in range(2):
            b = 2 * g + i
            dot_ref[b : b + 1, :] = dots[:, i * LANES : (i + 1) * LANES]
            one, two = (norm, turned) if i == 0 else (turned, norm)
            for t in range(HEADS // 2):
                norm_ref[b : b + 1, t * HEAD : (t + 1) * HEAD] = jnp.where(
                    left, one[2 * t : 2 * t + 1], two[2 * t + 1 : 2 * t + 2]
                )
            for h in range(HEADS):
                to = slice(b * LANES + h * BLOCK, b * LANES + (h + 1) * BLOCK)
                q_ref[to, :] = p_ref[i * BLOCK : (i + 1) * BLOCK, head(h)]
                do_ref[to, :] = p_ref[ROWS + i * BLOCK : ROWS + (i + 1) * BLOCK, head(h)]


def terms(
    work_ref, held_ref, place_ref, first_ref, own_ref, p0_ref, p1_ref, p2_ref, p3_ref, kv_ref,
    dq0_ref, dq1_ref, dq2_ref, dq3_ref, dkv_ref,
    acc_ref, half_ref, dqt_ref, own_buf, send_buf, q_ref, do_ref, norm_ref, dot_ref, sem,
):
    acc_ref[...] = jnp.zeros_like(acc_ref)
    dqt_ref[...] = jnp.zeros_like(dqt_ref)
    stage((p0_ref, p1_ref, p2_ref, p3_ref), q_ref, do_ref, norm_ref, dot_ref)

    def one(t):
        b, j = work_ref[t], work_ref[SLOTS + t]
        a0 = pl.multiple_of(place_ref[j], BLOCK)
        a1 = pl.multiple_of(place_ref[j + 1], BLOCK)
        rows = pl.ds(pl.multiple_of(b * LANES, LANES), LANES)
        q, do = q_ref[rows, :], do_ref[rows, :]
        k = jnp.concatenate([kv_ref[pl.ds(a0, BLOCK), :], kv_ref[pl.ds(a1, BLOCK), :]], 0)
        v = jnp.concatenate(
            [kv_ref[pl.ds(a0 + ROWS, BLOCK), :], kv_ref[pl.ds(a1 + ROWS, BLOCK), :]], 0
        )
        s = lax.dot_general(k, q, NT, preferred_element_type=jnp.float32)
        dp = lax.dot_general(v, do, NT, preferred_element_type=jnp.float32)
        lane = lax.broadcasted_iota(jnp.int32, (BLOCK, LANES), 0)
        pos = jnp.concatenate([lane + held_ref[j] * BLOCK, lane + held_ref[j + 1] * BLOCK], 0)
        at = pl.ds(b, 1)
        ok = (pos >= first_ref[at, :]) & (pos <= own_ref[at, :])
        w = jnp.where(ok, jnp.exp2(s * (SCALE * LOG2E) - norm_ref[at, :]), 0.0)
        ds = (w * (dp - dot_ref[at, :]) * SCALE).astype(jnp.bfloat16)
        dv = jnp.dot(w.astype(jnp.bfloat16), do, preferred_element_type=jnp.float32)
        dk = jnp.dot(ds, q, preferred_element_type=jnp.float32)
        dqt = lax.dot_general(k, ds, TN, preferred_element_type=jnp.float32)
        return b, a0, a1, dqt, dk, dv

    def two(i, carry):
        for b, a0, a1, dqt, dk, dv in [one(2 * i), one(2 * i + 1)]:
            dqt_ref[pl.ds(pl.multiple_of(b * HEAD, HEAD), HEAD), :] += dqt
            acc_ref[pl.ds(a0, BLOCK), :] += dk[:BLOCK]
            acc_ref[pl.ds(a1, BLOCK), :] += dk[BLOCK:]
            acc_ref[pl.ds(a0 + ROWS, BLOCK), :] += dv[:BLOCK]
            acc_ref[pl.ds(a1 + ROWS, BLOCK), :] += dv[BLOCK:]
        return carry

    lax.fori_loop(0, work_ref[2 * SLOTS], two, 0)
    copies = []
    for i in range(4):
        at = pl.ds(i * PEERS * BLOCK, PEERS * BLOCK)
        half_ref[at, :] = acc_ref[at, :].astype(jnp.bfloat16)
        copies.append(pltpu.make_async_copy(half_ref.at[at], dkv_ref.at[at], sem.at[i]))
        copies[-1].start()
    for g in (3, 2, 1, 0):
        out = send_buf.at[g - 1] if g else own_buf
        for i in range(2):
            b = 2 * g + i
            dq = dqt_ref[b * HEAD : (b + 1) * HEAD, :].T.astype(out.dtype)
            for h in range(HEADS):
                out[i * BLOCK : (i + 1) * BLOCK, head(h)] = dq[h * BLOCK : (h + 1) * BLOCK]
        to = (dq0_ref, dq1_ref, dq2_ref, dq3_ref)[g]
        copies.append(pltpu.make_async_copy(out, to, sem.at[4 + g]))
        copies[-1].start()
    for copy in copies:
        copy.wait()


def total(got_ref, k_ref, v_ref):
    both = got_ref[0].astype(jnp.float32)
    for i in range(1, PEERS):
        both = both + got_ref[i].astype(jnp.float32)
    k_ref[...] = both[:ROWS].astype(jnp.bfloat16)
    v_ref[...] = both[ROWS:].astype(jnp.bfloat16)


def plan(doc_lengths, block_order, yh, xh, xl, core):
    docs, nblk = doc_lengths.shape[0], block_order.shape[0]
    nheld = nblk // 4
    upto = jnp.arange(docs)[:, None] >= jnp.arange(docs)[None, :]
    ends = jnp.sum(jnp.where(upto, doc_lengths[None, :], 0), axis=1)
    blocks = jnp.arange(nblk, dtype=jnp.int32)
    held_here = ((blocks // 2) % 2 == core) & ((blocks // 4) % 2 == xl)
    place = (blocks // 8) * (2 * ROWS) + (blocks % 2) * BLOCK
    before = held_here[None, :] & (block_order[None, :] < block_order[:, None])
    rank = jnp.sum(before.astype(jnp.int32), axis=1)
    slots = jnp.arange(nheld + 8, dtype=jnp.int32)
    hit = held_here[None, :] & (rank[None, :] == slots[:, None])
    held = jnp.sum(jnp.where(hit, block_order[None, :], 0), axis=1)
    held = jnp.where(slots < nheld, held, nblk)
    place = jnp.sum(jnp.where(hit, place[None, :], 0), axis=1)
    x, turn = 2 * xh + xl, 1 - 2 * core
    owners = 8 * yh + jnp.stack(
        [
            2 * x + core,
            2 * x + 1 - core,
            2 * ((x + turn) % 4) + core,
            2 * ((x - turn) % 4) + 1 - core,
        ]
    )
    stored = (2 * owners[:, None] + jnp.arange(2)[None, :]).reshape(8)
    mine = jnp.sum(jnp.where(stored[:, None] == blocks[None, :], block_order[None, :], 0), axis=1)
    pos = mine[:, None] * BLOCK + jnp.arange(BLOCK, dtype=jnp.int32)[None, :]
    first = jnp.max(jnp.where(ends[None, None, :] <= pos[:, :, None], ends[None, None, :], 0), axis=2)
    begin = jnp.sum((held[None, :] < (first[:, :1] >> 6)).astype(jnp.int32), axis=1)
    until = jnp.sum((held[None, :] <= mine[:, None]).astype(jnp.int32), axis=1)
    pairs = (until - begin + 1) >> 1
    eight = jnp.arange(8)
    stops = jnp.sum(jnp.where(eight[:, None] >= eight[None, :], pairs[None, :], 0), axis=1)
    place_in = jnp.arange(SLOTS, dtype=jnp.int32)
    done = stops[None, :] <= place_in[:, None]
    of = jnp.sum(done.astype(jnp.int32), axis=1)
    this = of[:, None] == eight[None, :]
    at = jnp.sum(jnp.where(this, begin[None, :] - 2 * (stops - pairs)[None, :], 0), axis=1)
    at = jnp.where(of < 8, at + 2 * place_in, nheld)
    work = jnp.concatenate([jnp.minimum(of, 7), at, (stops[-1:] + 1) >> 1])
    return work, held, place, jnp.tile(first, (1, HEADS)), jnp.tile(pos, (1, HEADS))


def on_device(queries, keys, values, attn_out, grad_out, log_norm, doc_lengths, block_order):
    f32, bf16 = jnp.float32, jnp.bfloat16
    shape = jax.ShapeDtypeStruct
    place = [lax.axis_index(a) for a in CTX]
    dma = pltpu.SemaphoreType.DMA

    swap = [(0, 1), (1, 0)]
    there = [(2 * ((i + 1) % 4), 2 * i) for i in range(4)]
    there += [(2 * i + 1, 2 * ((i + 1) % 4) + 1) for i in range(4)]
    back = [(j, i) for i, j in there]
    across = [(2 * i, 2 * ((i - 1) % 4) + 1) for i in range(4)]
    across += [(2 * i + 1, 2 * ((i + 1) % 4)) for i in range(4)]
    sent, p0 = call(
        pack,
        (pltpu.HBM((PEERS, 2 * ROWS, HEAD), bf16), shape((2 * ROWS + EXTRA, WIDTH), bf16)),
        [HBM] * 6,
        (HBM, VMEM),
        *map(in_hbm, (keys, values, queries, grad_out, attn_out, log_norm)),
        scratch=[
            pltpu.VMEM((2 * ROWS, HEAD), bf16),
            pltpu.VMEM((ROWS, WIDTH), bf16),
            pltpu.VMEM((HEADS, ROWS), f32),
            dma((6,)),
            dma((PEERS,)),
        ],
    )
    kv = lax.all_to_all(sent, KEEPERS, 0, 0, tiled=True)
    p2 = lax.ppermute(p0, NEXT, there)
    p3 = lax.ppermute(p2, "core", swap)
    work, held, at, first, own = plan(doc_lengths, block_order, *place)
    later, held = lax.optimization_barrier((p0, held))
    p1 = lax.ppermute(later, "core", swap)
    nkeys = 2 * PEERS * ROWS
    dq0, *others, dkv = call(
        terms,
        (pltpu.HBM((ROWS, WIDTH), f32),)
        + (pltpu.HBM((ROWS, WIDTH), bf16),) * 3
        + (pltpu.HBM((nkeys, HEAD), bf16),),
        [SMEM] * 3 + [VMEM] * 7,
        (HBM,) * 5,
        work, held, at, first, own, p0, p1, p2, p3, kv.reshape(nkeys, HEAD),
        scratch=[
            pltpu.VMEM((nkeys, HEAD), f32),
            pltpu.VMEM((nkeys, HEAD), bf16),
            pltpu.VMEM((8 * HEAD, LANES), f32),
            pltpu.VMEM((ROWS, WIDTH), f32),
            pltpu.VMEM((3, ROWS, WIDTH), bf16),
            pltpu.VMEM((8 * LANES, HEAD), bf16),
            pltpu.VMEM((8 * LANES, HEAD), bf16),
            pltpu.VMEM((8, LANES), f32),
            pltpu.VMEM((8, LANES), f32),
            dma((8,)),
        ],
    )
    got = lax.all_to_all(dkv.reshape(PEERS, 2 * ROWS, HEAD), KEEPERS, 0, 0, tiled=True)
    routes = ((NEXT, across), (NEXT, back), ("core", swap))
    parts = [lax.ppermute(x, axes, route) for x, (axes, route) in zip(others[::-1], routes)]
    grad_q = (dq0 + sum(x.astype(f32) for x in parts)).astype(bf16)
    grad_k, grad_v = call(total, (shape((ROWS, HEAD), bf16),) * 2, [VMEM], (VMEM,) * 2, got)
    return grad_q, grad_k, grad_v


def solution(mesh):
    parts = Mesh(
        mesh.devices.reshape(2, 4, 2, 2, 2, 8), ("dp", "yh", "xh", "xl", "core", "tensor")
    )
    seq = ("dp",) + CTX
    wide = P(seq, "tensor")
    return jax.shard_map(
        on_device,
        mesh=parts,
        in_specs=(wide,) * 5 + (P("tensor", seq), P("dp"), P("dp")),
        out_specs=(wide, wide, wide),
        check_vma=False,
    )
```

```python
import math

import jax
import jax.numpy as jnp
from jax import lax
from jax.experimental import pallas as pl
from jax.experimental.pallas import tpu as pltpu
from jax.sharding import Mesh
from jax.sharding import PartitionSpec as P

HEADS = 8
HEAD = 128
BLOCK = 64
ROWS = 2 * BLOCK
WIDTH = HEADS * HEAD
LANES = HEADS * BLOCK
EXTRA = 16
PEERS = 8
SLOTS = 72
SCALE = 1.0 / math.sqrt(HEAD)
LOG2E = math.log2(math.e)
CTX = ("yh", "xh", "xl", "core")
KEEPERS = ("yh", "xl")
NEXT = ("xh", "xl", "core")
NT = (((1,), (1,)), ((), ()))
TN = (((0,), (0,)), ((), ()))
VMEM = pl.BlockSpec(memory_space=pltpu.VMEM)
SMEM = pl.BlockSpec(memory_space=pltpu.SMEM)
HBM = pl.BlockSpec(memory_space=pltpu.HBM)


def head(h):
    return slice(h * HEAD, (h + 1) * HEAD)


def in_hbm(x):
    return pltpu.with_memory_space_constraint(x, pltpu.HBM)


def call(kernel, out, ins, outs, *args, scratch=(), limit=16):
    return pl.pallas_call(
        kernel,
        out_shape=out,
        in_specs=ins,
        out_specs=outs,
        scratch_shapes=scratch,
        compiler_params=pltpu.CompilerParams(vmem_limit_bytes=limit << 20),
        name=kernel.__name__,
    )(*args)


def terms_of(x):
    parts = []
    for _ in range(3):
        term = x.astype(jnp.bfloat16).astype(jnp.float32)
        parts.append(term)
        x = x - term
    return parts


def pack(
    k_ref, v_ref, q_ref, do_ref, o_ref, norm_ref,
    kv_ref, out_ref, kv_buf, o_buf, norm_buf, sem, kv_sem,
):
    reads = [
        pltpu.make_async_copy(k_ref, kv_buf.at[:ROWS], sem.at[0]),
        pltpu.make_async_copy(v_ref, kv_buf.at[ROWS:], sem.at[1]),
        pltpu.make_async_copy(do_ref, out_ref.at[ROWS : 2 * ROWS], sem.at[2]),
        pltpu.make_async_copy(o_ref, o_buf, sem.at[3]),
        pltpu.make_async_copy(norm_ref, norm_buf, sem.at[4]),
        pltpu.make_async_copy(q_ref, out_ref.at[:ROWS], sem.at[5]),
    ]
    for copy in reads:
        copy.start()
    for copy in reads[:2]:
        copy.wait()
    writes = [pltpu.make_async_copy(kv_buf, kv_ref.at[i], kv_sem.at[i]) for i in range(PEERS)]
    for copy in writes:
        copy.start()
    for copy in reads[2:5]:
        copy.wait()
    ones = jnp.ones((8, HEAD), jnp.float32)
    dots = []
    for b in range(2):
        at = slice(b * BLOCK, (b + 1) * BLOCK)
        at2 = slice(ROWS + b * BLOCK, ROWS + (b + 1) * BLOCK)
        prod = jnp.concatenate(
            [
                out_ref[at2, head(h)].astype(jnp.float32) * o_buf[at, head(h)].astype(jnp.float32)
                for h in range(HEADS)
            ],
            0,
        )
        dots.append(
            lax.dot_general(
                ones, prod, NT, precision=lax.Precision.HIGHEST, preferred_element_type=jnp.float32
            )[:1]
        )
    norms = terms_of(norm_buf[...])
    norms = jnp.concatenate(norms + [jnp.zeros((8, WIDTH - 3 * HEAD), jnp.float32)], 1)
    dots = terms_of(jnp.concatenate(dots, 1))
    dots = dots + [jnp.zeros((5, WIDTH), jnp.float32)]
    out_ref[2 * ROWS :] = jnp.concatenate([norms] + dots, 0).astype(jnp.bfloat16)
    reads[5].wait()
    for copy in writes:
        copy.wait()


def stage(p_refs, q_ref, do_ref, norm_ref, dot_ref):
    for g, p_ref in enumerate(p_refs):
        more = p_ref[2 * ROWS :, :].astype(jnp.float32)
        norm = (more[:8, head(0)] + more[:8, head(1)] + more[:8, head(2)]) * LOG2E
        turned = pltpu.roll(norm, BLOCK, 1)
        left = lax.broadcasted_iota(jnp.int32, (1, HEAD), 1) < BLOCK
        dots = more[8:9] + more[9:10] + more[10:11]
        for i in range(2):
            b = 2 * g + i
            dot_ref[b : b + 1, :] = dots[:, i * LANES : (i + 1) * LANES]
            one, two = (norm, turned) if i == 0 else (turned, norm)
            for t in range(HEADS // 2):
                norm_ref[b : b + 1, t * HEAD : (t + 1) * HEAD] = jnp.where(
                    left, one[2 * t : 2 * t + 1], two[2 * t + 1 : 2 * t + 2]
                )
            for h in range(HEADS):
                to = slice(b * LANES + h * BLOCK, b * LANES + (h + 1) * BLOCK)
                q_ref[to, :] = p_ref[i * BLOCK : (i + 1) * BLOCK, head(h)]
                do_ref[to, :] = p_ref[ROWS + i * BLOCK : ROWS + (i + 1) * BLOCK, head(h)]


def terms(
    work_ref, held_ref, place_ref, first_ref, own_ref, p0_ref, p1_ref, p2_ref, p3_ref, kv_ref,
    dq0_ref, dq1_ref, dq2_ref, dq3_ref, dkv_ref,
    acc_ref, half_ref, dqt_ref, own_buf, send_buf, q_ref, do_ref, norm_ref, dot_ref, sem,
):
    acc_ref[...] = jnp.zeros_like(acc_ref)
    dqt_ref[...] = jnp.zeros_like(dqt_ref)
    stage((p0_ref, p1_ref, p2_ref, p3_ref), q_ref, do_ref, norm_ref, dot_ref)

    def one(t):
        b, j = work_ref[t], work_ref[SLOTS + t]
        a0 = pl.multiple_of(place_ref[j], BLOCK)
        a1 = pl.multiple_of(place_ref[j + 1], BLOCK)
        rows = pl.ds(pl.multiple_of(b * LANES, LANES), LANES)
        q, do = q_ref[rows, :], do_ref[rows, :]
        k = jnp.concatenate([kv_ref[pl.ds(a0, BLOCK), :], kv_ref[pl.ds(a1, BLOCK), :]], 0)
        v = jnp.concatenate(
            [kv_ref[pl.ds(a0 + ROWS, BLOCK), :], kv_ref[pl.ds(a1 + ROWS, BLOCK), :]], 0
        )
        s = lax.dot_general(k, q, NT, preferred_element_type=jnp.float32)
        dp = lax.dot_general(v, do, NT, preferred_element_type=jnp.float32)
        lane = lax.broadcasted_iota(jnp.int32, (BLOCK, LANES), 0)
        pos = jnp.concatenate([lane + held_ref[j] * BLOCK, lane + held_ref[j + 1] * BLOCK], 0)
        at = pl.ds(b, 1)
        ok = (pos >= first_ref[at, :]) & (pos <= own_ref[at, :])
        w = jnp.where(ok, jnp.exp2(s * (SCALE * LOG2E) - norm_ref[at, :]), 0.0)
        ds = (w * (dp - dot_ref[at, :]) * SCALE).astype(jnp.bfloat16)
        dv = jnp.dot(w.astype(jnp.bfloat16), do, preferred_element_type=jnp.float32)
        dk = jnp.dot(ds, q, preferred_element_type=jnp.float32)
        dqt = lax.dot_general(k, ds, TN, preferred_element_type=jnp.float32)
        return b, a0, a1, dqt, dk, dv

    def two(i, carry):
        for b, a0, a1, dqt, dk, dv in [one(2 * i), one(2 * i + 1)]:
            dqt_ref[pl.ds(pl.multiple_of(b * HEAD, HEAD), HEAD), :] += dqt
            acc_ref[pl.ds(a0, BLOCK), :] += dk[:BLOCK]
            acc_ref[pl.ds(a1, BLOCK), :] += dk[BLOCK:]
            acc_ref[pl.ds(a0 + ROWS, BLOCK), :] += dv[:BLOCK]
            acc_ref[pl.ds(a1 + ROWS, BLOCK), :] += dv[BLOCK:]
        return carry

    lax.fori_loop(0, work_ref[2 * SLOTS], two, 0)
    copies = []
    for i in range(4):
        at = pl.ds(i * PEERS * BLOCK, PEERS * BLOCK)
        half_ref[at, :] = acc_ref[at, :].astype(jnp.bfloat16)
        copies.append(pltpu.make_async_copy(half_ref.at[at], dkv_ref.at[at], sem.at[i]))
        copies[-1].start()
    for g in (3, 2, 1, 0):
        out = send_buf.at[g - 1] if g else own_buf
        for i in range(2):
            b = 2 * g + i
            dq = dqt_ref[b * HEAD : (b + 1) * HEAD, :].T.astype(out.dtype)
            for h in range(HEADS):
                out[i * BLOCK : (i + 1) * BLOCK, head(h)] = dq[h * BLOCK : (h + 1) * BLOCK]
        to = (dq0_ref, dq1_ref, dq2_ref, dq3_ref)[g]
        copies.append(pltpu.make_async_copy(out, to, sem.at[4 + g]))
        copies[-1].start()
    for copy in copies:
        copy.wait()


def finish(got_ref, own_ref, a_ref, b_ref, c_ref, dq_ref, k_ref, v_ref):
    f32, bf16 = jnp.float32, jnp.bfloat16
    both = got_ref[0].astype(f32)
    for i in range(1, PEERS):
        both = both + got_ref[i].astype(f32)
    k_ref[...] = both[:ROWS].astype(bf16)
    v_ref[...] = both[ROWS:].astype(bf16)
    parts = a_ref[...].astype(f32) + b_ref[...].astype(f32) + c_ref[...].astype(f32)
    dq_ref[...] = (own_ref[...] + parts).astype(bf16)


def plan(doc_lengths, block_order, yh, xh, xl, core):
    docs, nblk = doc_lengths.shape[0], block_order.shape[0]
    nheld = nblk // 4
    upto = jnp.arange(docs)[:, None] >= jnp.arange(docs)[None, :]
    ends = jnp.sum(jnp.where(upto, doc_lengths[None, :], 0), axis=1)
    blocks = jnp.arange(nblk, dtype=jnp.int32)
    held_here = ((blocks // 2) % 2 == core) & ((blocks // 8) % 2 == xh)
    place = ((blocks // 16) * 2 + (blocks // 4) % 2) * (2 * ROWS) + (blocks % 2) * BLOCK
    before = held_here[None, :] & (block_order[None, :] < block_order[:, None])
    rank = jnp.sum(before.astype(jnp.int32), axis=1)
    slots = jnp.arange(nheld + 8, dtype=jnp.int32)
    hit = held_here[None, :] & (rank[None, :] == slots[:, None])
    held = jnp.sum(jnp.where(hit, block_order[None, :], 0), axis=1)
    held = jnp.where(slots < nheld, held, nblk)
    place = jnp.sum(jnp.where(hit, place[None, :], 0), axis=1)
    x = 2 * xh + xl
    partner = (x + 2 * xl - 1) % 4
    owners = 8 * yh + jnp.stack(
        [2 * x + core, 2 * x + 1 - core, 2 * partner + core, 2 * partner + 1 - core]
    )
    stored = (2 * owners[:, None] + jnp.arange(2)[None, :]).reshape(8)
    mine = jnp.sum(jnp.where(stored[:, None] == blocks[None, :], block_order[None, :], 0), axis=1)
    pos = mine[:, None] * BLOCK + jnp.arange(BLOCK, dtype=jnp.int32)[None, :]
    first = jnp.max(jnp.where(ends[None, None, :] <= pos[:, :, None], ends[None, None, :], 0), axis=2)
    begin = jnp.sum((held[None, :] < (first[:, :1] >> 6)).astype(jnp.int32), axis=1)
    until = jnp.sum((held[None, :] <= mine[:, None]).astype(jnp.int32), axis=1)
    pairs = (until - begin + 1) >> 1
    eight = jnp.arange(8)
    stops = jnp.sum(jnp.where(eight[:, None] >= eight[None, :], pairs[None, :], 0), axis=1)
    place_in = jnp.arange(SLOTS, dtype=jnp.int32)
    done = stops[None, :] <= place_in[:, None]
    of = jnp.sum(done.astype(jnp.int32), axis=1)
    this = of[:, None] == eight[None, :]
    at = jnp.sum(jnp.where(this, begin[None, :] - 2 * (stops - pairs)[None, :], 0), axis=1)
    at = jnp.where(of < 8, at + 2 * place_in, nheld)
    work = jnp.concatenate([jnp.minimum(of, 7), at, (stops[-1:] + 1) >> 1])
    return work, held, place, jnp.tile(first, (1, HEADS)), jnp.tile(pos, (1, HEADS))


def on_device(queries, keys, values, attn_out, grad_out, log_norm, doc_lengths, block_order):
    f32, bf16 = jnp.float32, jnp.bfloat16
    shape = jax.ShapeDtypeStruct
    place = [lax.axis_index(a) for a in CTX]
    dma = pltpu.SemaphoreType.DMA

    swap = [(0, 1), (1, 0)]
    partner = [3, 2, 1, 0]
    facing = [(2 * i + c, 2 * partner[i] + c) for i in range(4) for c in range(2)]
    across = [(2 * i + c, 2 * partner[i] + 1 - c) for i in range(4) for c in range(2)]
    sent, p0 = call(
        pack,
        (pltpu.HBM((PEERS, 2 * ROWS, HEAD), bf16), shape((2 * ROWS + EXTRA, WIDTH), bf16)),
        [HBM] * 6,
        (HBM, VMEM),
        *map(in_hbm, (keys, values, queries, grad_out, attn_out, log_norm)),
        scratch=[
            pltpu.VMEM((2 * ROWS, HEAD), bf16),
            pltpu.VMEM((ROWS, WIDTH), bf16),
            pltpu.VMEM((HEADS, ROWS), f32),
            dma((6,)),
            dma((PEERS,)),
        ],
    )
    kv = lax.all_to_all(sent, KEEPERS, 0, 0, tiled=True)
    p2 = lax.ppermute(p0, NEXT, facing)
    p3 = lax.ppermute(p2, "core", swap)
    work, held, at, first, own = plan(doc_lengths, block_order, *place)
    later, held = lax.optimization_barrier((p0, held))
    p1 = lax.ppermute(later, "core", swap)
    nkeys = 2 * PEERS * ROWS
    dq0, *others, dkv = call(
        terms,
        (pltpu.HBM((ROWS, WIDTH), f32),)
        + (pltpu.HBM((ROWS, WIDTH), bf16),) * 3
        + (pltpu.HBM((nkeys, HEAD), bf16),),
        [SMEM] * 3 + [VMEM] * 7,
        (HBM,) * 5,
        work, held, at, first, own, p0, p1, p2, p3, kv.reshape(nkeys, HEAD),
        scratch=[
            pltpu.VMEM((nkeys, HEAD), f32),
            pltpu.VMEM((nkeys, HEAD), bf16),
            pltpu.VMEM((8 * HEAD, LANES), f32),
            pltpu.VMEM((ROWS, WIDTH), f32),
            pltpu.VMEM((3, ROWS, WIDTH), bf16),
            pltpu.VMEM((8 * LANES, HEAD), bf16),
            pltpu.VMEM((8 * LANES, HEAD), bf16),
            pltpu.VMEM((8, LANES), f32),
            pltpu.VMEM((8, LANES), f32),
            dma((8,)),
        ],
    )
    got = lax.all_to_all(dkv.reshape(PEERS, 2 * ROWS, HEAD), KEEPERS, 0, 0, tiled=True)
    routes = ((NEXT, across), (NEXT, facing), ("core", swap))
    parts = [lax.ppermute(x, axes, route) for x, (axes, route) in zip(others[::-1], routes)]
    grad_q, grad_k, grad_v = call(
        finish,
        (shape((ROWS, WIDTH), bf16),) + (shape((ROWS, HEAD), bf16),) * 2,
        [VMEM] * 5,
        (VMEM,) * 3,
        got, dq0, *parts,
    )
    return grad_q, grad_k, grad_v


def solution(mesh):
    parts = Mesh(
        mesh.devices.reshape(2, 4, 2, 2, 2, 8), ("dp", "yh", "xh", "xl", "core", "tensor")
    )
    seq = ("dp",) + CTX
    wide = P(seq, "tensor")
    return jax.shard_map(
        on_device,
        mesh=parts,
        in_specs=(wide,) * 5 + (P("tensor", seq), P("dp"), P("dp")),
        out_specs=(wide, wide, wide),
        check_vma=False,
    )
```

```python
import math

import jax
import jax.numpy as jnp
from jax import lax
from jax.experimental import pallas as pl
from jax.experimental.pallas import tpu as pltpu
from jax.sharding import Mesh
from jax.sharding import PartitionSpec as P

HEADS = 8
HEAD = 128
BLOCK = 64
ROWS = 2 * BLOCK
WIDTH = HEADS * HEAD
LANES = HEADS * BLOCK
EXTRA = 16
PEERS = 8
SLOTS = 72
SCALE = 1.0 / math.sqrt(HEAD)
LOG2E = math.log2(math.e)
CTX = ("yh", "xh", "xl", "core")
KEEPERS = ("yh", "xl")
NEXT = ("xh", "xl", "core")
NT = (((1,), (1,)), ((), ()))
TN = (((0,), (0,)), ((), ()))
VMEM = pl.BlockSpec(memory_space=pltpu.VMEM)
SMEM = pl.BlockSpec(memory_space=pltpu.SMEM)
HBM = pl.BlockSpec(memory_space=pltpu.HBM)


def head(h):
    return slice(h * HEAD, (h + 1) * HEAD)


def in_hbm(x):
    return pltpu.with_memory_space_constraint(x, pltpu.HBM)


def call(kernel, out, ins, outs, *args, scratch=(), limit=16):
    return pl.pallas_call(
        kernel,
        out_shape=out,
        in_specs=ins,
        out_specs=outs,
        scratch_shapes=scratch,
        compiler_params=pltpu.CompilerParams(vmem_limit_bytes=limit << 20),
        name=kernel.__name__,
    )(*args)


def terms_of(x):
    parts = []
    for _ in range(3):
        term = x.astype(jnp.bfloat16).astype(jnp.float32)
        parts.append(term)
        x = x - term
    return parts


def pack(
    k_ref, v_ref, q_ref, do_ref, o_ref, norm_ref,
    kv_ref, out_ref, kv_buf, o_buf, norm_buf, sem, kv_sem,
):
    reads = [
        pltpu.make_async_copy(k_ref, kv_buf.at[:ROWS], sem.at[0]),
        pltpu.make_async_copy(v_ref, kv_buf.at[ROWS:], sem.at[1]),
        pltpu.make_async_copy(do_ref, out_ref.at[ROWS : 2 * ROWS], sem.at[2]),
        pltpu.make_async_copy(o_ref, o_buf, sem.at[3]),
        pltpu.make_async_copy(norm_ref, norm_buf, sem.at[4]),
        pltpu.make_async_copy(q_ref, out_ref.at[:ROWS], sem.at[5]),
    ]
    for copy in reads:
        copy.start()
    for copy in reads[:2]:
        copy.wait()
    writes = [pltpu.make_async_copy(kv_buf, kv_ref.at[i], kv_sem.at[i]) for i in range(PEERS)]
    for copy in writes:
        copy.start()
    for copy in reads[2:5]:
        copy.wait()
    ones = jnp.ones((8, HEAD), jnp.float32)
    dots = []
    for b in range(2):
        at = slice(b * BLOCK, (b + 1) * BLOCK)
        at2 = slice(ROWS + b * BLOCK, ROWS + (b + 1) * BLOCK)
        prod = jnp.concatenate(
            [
                out_ref[at2, head(h)].astype(jnp.float32) * o_buf[at, head(h)].astype(jnp.float32)
                for h in range(HEADS)
            ],
            0,
        )
        dots.append(
            lax.dot_general(
                ones, prod, NT, precision=lax.Precision.HIGHEST, preferred_element_type=jnp.float32
            )[:1]
        )
    norms = terms_of(norm_buf[...])
    norms = jnp.concatenate(norms + [jnp.zeros((8, WIDTH - 3 * HEAD), jnp.float32)], 1)
    dots = terms_of(jnp.concatenate(dots, 1))
    dots = dots + [jnp.zeros((5, WIDTH), jnp.float32)]
    out_ref[2 * ROWS :] = jnp.concatenate([norms] + dots, 0).astype(jnp.bfloat16)
    reads[5].wait()
    for copy in writes:
        copy.wait()


def stage(p_refs, q_ref, do_ref, norm_ref, dot_ref):
    for g, p_ref in enumerate(p_refs):
        more = p_ref[2 * ROWS :, :].astype(jnp.float32)
        norm = (more[:8, head(0)] + more[:8, head(1)] + more[:8, head(2)]) * LOG2E
        turned = pltpu.roll(norm, BLOCK, 1)
        left = lax.broadcasted_iota(jnp.int32, (1, HEAD), 1) < BLOCK
        dots = more[8:9] + more[9:10] + more[10:11]
        for i in range(2):
            b = 2 * g + i
            dot_ref[b : b + 1, :] = dots[:, i * LANES : (i + 1) * LANES]
            one, two = (norm, turned) if i == 0 else (turned, norm)
            for t in range(HEADS // 2):
                norm_ref[b : b + 1, t * HEAD : (t + 1) * HEAD] = jnp.where(
                    left, one[2 * t : 2 * t + 1], two[2 * t + 1 : 2 * t + 2]
                )
            for h in range(HEADS):
                to = slice(b * LANES + h * BLOCK, b * LANES + (h + 1) * BLOCK)
                q_ref[to, :] = p_ref[i * BLOCK : (i + 1) * BLOCK, head(h)]
                do_ref[to, :] = p_ref[ROWS + i * BLOCK : ROWS + (i + 1) * BLOCK, head(h)]


def terms(
    work_ref, held_ref, place_ref, first_ref, own_ref, p0_ref, p1_ref, p2_ref, p3_ref, kv_ref,
    dq0_ref, dq2_ref, side_ref, dkv_ref,
    acc_ref, half_ref, dqt_ref, keep_buf, side_buf, q_ref, do_ref, norm_ref, dot_ref, sem,
):
    acc_ref[...] = jnp.zeros_like(acc_ref)
    dqt_ref[...] = jnp.zeros_like(dqt_ref)
    stage((p0_ref, p1_ref, p2_ref, p3_ref), q_ref, do_ref, norm_ref, dot_ref)

    def one(t):
        b, j = work_ref[t], work_ref[SLOTS + t]
        a0 = pl.multiple_of(place_ref[j], BLOCK)
        a1 = pl.multiple_of(place_ref[j + 1], BLOCK)
        rows = pl.ds(pl.multiple_of(b * LANES, LANES), LANES)
        q, do = q_ref[rows, :], do_ref[rows, :]
        k = jnp.concatenate([kv_ref[pl.ds(a0, BLOCK), :], kv_ref[pl.ds(a1, BLOCK), :]], 0)
        v = jnp.concatenate(
            [kv_ref[pl.ds(a0 + ROWS, BLOCK), :], kv_ref[pl.ds(a1 + ROWS, BLOCK), :]], 0
        )
        s = lax.dot_general(k, q, NT, preferred_element_type=jnp.float32)
        dp = lax.dot_general(v, do, NT, preferred_element_type=jnp.float32)
        lane = lax.broadcasted_iota(jnp.int32, (BLOCK, LANES), 0)
        pos = jnp.concatenate([lane + held_ref[j] * BLOCK, lane + held_ref[j + 1] * BLOCK], 0)
        at = pl.ds(b, 1)
        ok = (pos >= first_ref[at, :]) & (pos <= own_ref[at, :])
        w = jnp.where(ok, jnp.exp2(s * (SCALE * LOG2E) - norm_ref[at, :]), 0.0)
        ds = (w * (dp - dot_ref[at, :]) * SCALE).astype(jnp.bfloat16)
        dv = jnp.dot(w.astype(jnp.bfloat16), do, preferred_element_type=jnp.float32)
        dk = jnp.dot(ds, q, preferred_element_type=jnp.float32)
        dqt = lax.dot_general(k, ds, TN, preferred_element_type=jnp.float32)
        return b, a0, a1, dqt, dk, dv

    def two(i, carry):
        for b, a0, a1, dqt, dk, dv in [one(2 * i), one(2 * i + 1)]:
            dqt_ref[pl.ds(pl.multiple_of(b * HEAD, HEAD), HEAD), :] += dqt
            acc_ref[pl.ds(a0, BLOCK), :] += dk[:BLOCK]
            acc_ref[pl.ds(a1, BLOCK), :] += dk[BLOCK:]
            acc_ref[pl.ds(a0 + ROWS, BLOCK), :] += dv[:BLOCK]
            acc_ref[pl.ds(a1 + ROWS, BLOCK), :] += dv[BLOCK:]
        return carry

    lax.fori_loop(0, work_ref[2 * SLOTS], two, 0)
    copies = []
    for i in range(4):
        at = pl.ds(i * PEERS * BLOCK, PEERS * BLOCK)
        half_ref[at, :] = acc_ref[at, :].astype(jnp.bfloat16)
        copies.append(pltpu.make_async_copy(half_ref.at[at], dkv_ref.at[at], sem.at[i]))
        copies[-1].start()
    for g in (1, 3, 2, 0):
        buf, to = (side_buf, side_ref) if g % 2 else (keep_buf, (dq0_ref, dq2_ref)[g // 2])
        for i in range(2):
            b = 2 * g + i
            dq = dqt_ref[b * HEAD : (b + 1) * HEAD, :].T.astype(buf.dtype)
            for h in range(HEADS):
                buf[g // 2, i * BLOCK : (i + 1) * BLOCK, head(h)] = dq[h * BLOCK : (h + 1) * BLOCK]
        to = to.at[g // 2] if g % 2 else to
        copies.append(pltpu.make_async_copy(buf.at[g // 2], to, sem.at[4 + g]))
        copies[-1].start()
    for copy in copies:
        copy.wait()


def pass_on(dq_ref, side_ref, out_ref):
    out_ref[...] = (dq_ref[...] + side_ref[1].astype(jnp.float32)).astype(jnp.bfloat16)


def finish(got_ref, own_ref, side_ref, far_ref, dq_ref, k_ref, v_ref):
    f32, bf16 = jnp.float32, jnp.bfloat16
    both = got_ref[0].astype(f32)
    for i in range(1, PEERS):
        both = both + got_ref[i].astype(f32)
    k_ref[...] = both[:ROWS].astype(bf16)
    v_ref[...] = both[ROWS:].astype(bf16)
    parts = side_ref[0].astype(f32) + far_ref[...].astype(f32)
    dq_ref[...] = (own_ref[...] + parts).astype(bf16)


def plan(doc_lengths, block_order, yh, xh, xl, core):
    docs, nblk = doc_lengths.shape[0], block_order.shape[0]
    nheld = nblk // 4
    upto = jnp.arange(docs)[:, None] >= jnp.arange(docs)[None, :]
    ends = jnp.sum(jnp.where(upto, doc_lengths[None, :], 0), axis=1)
    blocks = jnp.arange(nblk, dtype=jnp.int32)
    held_here = ((blocks // 2) % 2 == core) & ((blocks // 8) % 2 == xh)
    place = ((blocks // 16) * 2 + (blocks // 4) % 2) * (2 * ROWS) + (blocks % 2) * BLOCK
    before = held_here[None, :] & (block_order[None, :] < block_order[:, None])
    rank = jnp.sum(before.astype(jnp.int32), axis=1)
    slots = jnp.arange(nheld + 8, dtype=jnp.int32)
    hit = held_here[None, :] & (rank[None, :] == slots[:, None])
    held = jnp.sum(jnp.where(hit, block_order[None, :], 0), axis=1)
    held = jnp.where(slots < nheld, held, nblk)
    place = jnp.sum(jnp.where(hit, place[None, :], 0), axis=1)
    x = 2 * xh + xl
    partner = (x + 2 * xl - 1) % 4
    owners = 8 * yh + jnp.stack(
        [2 * x + core, 2 * x + 1 - core, 2 * partner + core, 2 * partner + 1 - core]
    )
    stored = (2 * owners[:, None] + jnp.arange(2)[None, :]).reshape(8)
    mine = jnp.sum(jnp.where(stored[:, None] == blocks[None, :], block_order[None, :], 0), axis=1)
    pos = mine[:, None] * BLOCK + jnp.arange(BLOCK, dtype=jnp.int32)[None, :]
    first = jnp.max(jnp.where(ends[None, None, :] <= pos[:, :, None], ends[None, None, :], 0), axis=2)
    begin = jnp.sum((held[None, :] < (first[:, :1] >> 6)).astype(jnp.int32), axis=1)
    until = jnp.sum((held[None, :] <= mine[:, None]).astype(jnp.int32), axis=1)
    pairs = (until - begin + 1) >> 1
    eight = jnp.arange(8)
    stops = jnp.sum(jnp.where(eight[:, None] >= eight[None, :], pairs[None, :], 0), axis=1)
    place_in = jnp.arange(SLOTS, dtype=jnp.int32)
    done = stops[None, :] <= place_in[:, None]
    of = jnp.sum(done.astype(jnp.int32), axis=1)
    this = of[:, None] == eight[None, :]
    at = jnp.sum(jnp.where(this, begin[None, :] - 2 * (stops - pairs)[None, :], 0), axis=1)
    at = jnp.where(of < 8, at + 2 * place_in, nheld)
    work = jnp.concatenate([jnp.minimum(of, 7), at, (stops[-1:] + 1) >> 1])
    return work, held, place, jnp.tile(first, (1, HEADS)), jnp.tile(pos, (1, HEADS))


def on_device(queries, keys, values, attn_out, grad_out, log_norm, doc_lengths, block_order):
    f32, bf16 = jnp.float32, jnp.bfloat16
    shape = jax.ShapeDtypeStruct
    place = [lax.axis_index(a) for a in CTX]
    dma = pltpu.SemaphoreType.DMA

    swap = [(0, 1), (1, 0)]
    partner = [3, 2, 1, 0]
    facing = [(2 * i + c, 2 * partner[i] + c) for i in range(4) for c in range(2)]
    sent, p0 = call(
        pack,
        (pltpu.HBM((PEERS, 2 * ROWS, HEAD), bf16), shape((2 * ROWS + EXTRA, WIDTH), bf16)),
        [HBM] * 6,
        (HBM, VMEM),
        *map(in_hbm, (keys, values, queries, grad_out, attn_out, log_norm)),
        scratch=[
            pltpu.VMEM((2 * ROWS, HEAD), bf16),
            pltpu.VMEM((ROWS, WIDTH), bf16),
            pltpu.VMEM((HEADS, ROWS), f32),
            dma((6,)),
            dma((PEERS,)),
        ],
    )
    kv = lax.all_to_all(sent, KEEPERS, 0, 0, tiled=True)
    p2 = lax.ppermute(p0, NEXT, facing)
    p3 = lax.ppermute(p2, "core", swap)
    work, held, at, first, own = plan(doc_lengths, block_order, *place)
    later, held = lax.optimization_barrier((p0, held))
    p1 = lax.ppermute(later, "core", swap)
    nkeys = 2 * PEERS * ROWS
    dq0, dq2, side, dkv = call(
        terms,
        (pltpu.HBM((ROWS, WIDTH), f32),) * 2
        + (pltpu.HBM((2, ROWS, WIDTH), bf16), pltpu.HBM((nkeys, HEAD), bf16)),
        [SMEM] * 3 + [VMEM] * 7,
        (HBM,) * 4,
        work, held, at, first, own, p0, p1, p2, p3, kv.reshape(nkeys, HEAD),
        scratch=[
            pltpu.VMEM((nkeys, HEAD), f32),
            pltpu.VMEM((nkeys, HEAD), bf16),
            pltpu.VMEM((8 * HEAD, LANES), f32),
            pltpu.VMEM((2, ROWS, WIDTH), f32),
            pltpu.VMEM((2, ROWS, WIDTH), bf16),
            pltpu.VMEM((8 * LANES, HEAD), bf16),
            pltpu.VMEM((8 * LANES, HEAD), bf16),
            pltpu.VMEM((8, LANES), f32),
            pltpu.VMEM((8, LANES), f32),
            dma((8,)),
        ],
    )
    got = lax.all_to_all(dkv.reshape(PEERS, 2 * ROWS, HEAD), KEEPERS, 0, 0, tiled=True)
    side = lax.ppermute(side, "core", swap)
    far = call(pass_on, shape((ROWS, WIDTH), bf16), [VMEM] * 2, VMEM, dq2, side)
    far = lax.ppermute(far, NEXT, facing)
    grad_q, grad_k, grad_v = call(
        finish,
        (shape((ROWS, WIDTH), bf16),) + (shape((ROWS, HEAD), bf16),) * 2,
        [VMEM] * 4,
        (VMEM,) * 3,
        got, dq0, side, far,
    )
    return grad_q, grad_k, grad_v


def solution(mesh):
    parts = Mesh(
        mesh.devices.reshape(2, 4, 2, 2, 2, 8), ("dp", "yh", "xh", "xl", "core", "tensor")
    )
    seq = ("dp",) + CTX
    wide = P(seq, "tensor")
    return jax.shard_map(
        on_device,
        mesh=parts,
        in_specs=(wide,) * 5 + (P("tensor", seq), P("dp"), P("dp")),
        out_specs=(wide, wide, wide),
        check_vma=False,
    )
```

```python
import math

import jax
import jax.numpy as jnp
from jax import lax
from jax.experimental import pallas as pl
from jax.experimental.pallas import tpu as pltpu
from jax.sharding import Mesh
from jax.sharding import PartitionSpec as P

HEADS = 8
HEAD = 128
BLOCK = 64
ROWS = 2 * BLOCK
WIDTH = HEADS * HEAD
LANES = HEADS * BLOCK
EXTRA = 16
PEERS = 8
SLOTS = 72
SCALE = 1.0 / math.sqrt(HEAD)
LOG2E = math.log2(math.e)
CTX = ("yh", "xh", "xl", "core")
KEEPERS = ("yh", "xh")
NEXT = ("xh", "xl", "core")
NT = (((1,), (1,)), ((), ()))
TN = (((0,), (0,)), ((), ()))
VMEM = pl.BlockSpec(memory_space=pltpu.VMEM)
SMEM = pl.BlockSpec(memory_space=pltpu.SMEM)
HBM = pl.BlockSpec(memory_space=pltpu.HBM)


def head(h):
    return slice(h * HEAD, (h + 1) * HEAD)


def in_hbm(x):
    return pltpu.with_memory_space_constraint(x, pltpu.HBM)


def call(kernel, out, ins, outs, *args, scratch=(), limit=16):
    return pl.pallas_call(
        kernel,
        out_shape=out,
        in_specs=ins,
        out_specs=outs,
        scratch_shapes=scratch,
        compiler_params=pltpu.CompilerParams(vmem_limit_bytes=limit << 20),
        name=kernel.__name__,
    )(*args)


def terms_of(x):
    parts = []
    for _ in range(3):
        term = x.astype(jnp.bfloat16).astype(jnp.float32)
        parts.append(term)
        x = x - term
    return parts


def pack(
    k_ref, v_ref, q_ref, do_ref, o_ref, norm_ref,
    kv_ref, out_ref, kv_buf, o_buf, norm_buf, sem, kv_sem,
):
    reads = [
        pltpu.make_async_copy(k_ref, kv_buf.at[:ROWS], sem.at[0]),
        pltpu.make_async_copy(v_ref, kv_buf.at[ROWS:], sem.at[1]),
        pltpu.make_async_copy(do_ref, out_ref.at[ROWS : 2 * ROWS], sem.at[2]),
        pltpu.make_async_copy(o_ref, o_buf, sem.at[3]),
        pltpu.make_async_copy(norm_ref, norm_buf, sem.at[4]),
        pltpu.make_async_copy(q_ref, out_ref.at[:ROWS], sem.at[5]),
    ]
    for copy in reads:
        copy.start()
    for copy in reads[:2]:
        copy.wait()
    writes = [pltpu.make_async_copy(kv_buf, kv_ref.at[i], kv_sem.at[i]) for i in range(PEERS)]
    for copy in writes:
        copy.start()
    for copy in reads[2:5]:
        copy.wait()
    ones = jnp.ones((8, HEAD), jnp.float32)
    dots = []
    for b in range(2):
        at = slice(b * BLOCK, (b + 1) * BLOCK)
        at2 = slice(ROWS + b * BLOCK, ROWS + (b + 1) * BLOCK)
        prod = jnp.concatenate(
            [
                out_ref[at2, head(h)].astype(jnp.float32) * o_buf[at, head(h)].astype(jnp.float32)
                for h in range(HEADS)
            ],
            0,
        )
        dots.append(
            lax.dot_general(
                ones, prod, NT, precision=lax.Precision.HIGHEST, preferred_element_type=jnp.float32
            )[:1]
        )
    norms = terms_of(norm_buf[...])
    norms = jnp.concatenate(norms + [jnp.zeros((8, WIDTH - 3 * HEAD), jnp.float32)], 1)
    dots = terms_of(jnp.concatenate(dots, 1))
    dots = dots + [jnp.zeros((5, WIDTH), jnp.float32)]
    out_ref[2 * ROWS :] = jnp.concatenate([norms] + dots, 0).astype(jnp.bfloat16)
    reads[5].wait()
    for copy in writes:
        copy.wait()


def stage(p_refs, q_ref, do_ref, norm_ref, dot_ref):
    for g, p_ref in enumerate(p_refs):
        more = p_ref[2 * ROWS :, :].astype(jnp.float32)
        norm = (more[:8, head(0)] + more[:8, head(1)] + more[:8, head(2)]) * LOG2E
        turned = pltpu.roll(norm, BLOCK, 1)
        left = lax.broadcasted_iota(jnp.int32, (1, HEAD), 1) < BLOCK
        dots = more[8:9] + more[9:10] + more[10:11]
        for i in range(2):
            b = 2 * g + i
            dot_ref[b : b + 1, :] = dots[:, i * LANES : (i + 1) * LANES]
            one, two = (norm, turned) if i == 0 else (turned, norm)
            for t in range(HEADS // 2):
                norm_ref[b : b + 1, t * HEAD : (t + 1) * HEAD] = jnp.where(
                    left, one[2 * t : 2 * t + 1], two[2 * t + 1 : 2 * t + 2]
                )
            for h in range(HEADS):
                to = slice(b * LANES + h * BLOCK, b * LANES + (h + 1) * BLOCK)
                q_ref[to, :] = p_ref[i * BLOCK : (i + 1) * BLOCK, head(h)]
                do_ref[to, :] = p_ref[ROWS + i * BLOCK : ROWS + (i + 1) * BLOCK, head(h)]


def terms(
    work_ref, held_ref, place_ref, first_ref, own_ref, p0_ref, p1_ref, p2_ref, p3_ref, kv_ref,
    dq0_ref, dq2_ref, side_ref, dkv_ref,
    acc_ref, half_ref, dqt_ref, keep_buf, side_buf, q_ref, do_ref, norm_ref, dot_ref, sem,
):
    acc_ref[...] = jnp.zeros_like(acc_ref)
    dqt_ref[...] = jnp.zeros_like(dqt_ref)
    stage((p0_ref, p1_ref, p2_ref, p3_ref), q_ref, do_ref, norm_ref, dot_ref)

    def one(t):
        b, j = work_ref[t], work_ref[SLOTS + t]
        a0 = pl.multiple_of(place_ref[j], BLOCK)
        a1 = pl.multiple_of(place_ref[j + 1], BLOCK)
        rows = pl.ds(pl.multiple_of(b * LANES, LANES), LANES)
        q, do = q_ref[rows, :], do_ref[rows, :]
        k = jnp.concatenate([kv_ref[pl.ds(a0, BLOCK), :], kv_ref[pl.ds(a1, BLOCK), :]], 0)
        v = jnp.concatenate(
            [kv_ref[pl.ds(a0 + ROWS, BLOCK), :], kv_ref[pl.ds(a1 + ROWS, BLOCK), :]], 0
        )
        s = lax.dot_general(k, q, NT, preferred_element_type=jnp.float32)
        dp = lax.dot_general(v, do, NT, preferred_element_type=jnp.float32)
        lane = lax.broadcasted_iota(jnp.int32, (BLOCK, LANES), 0)
        pos = jnp.concatenate([lane + held_ref[j] * BLOCK, lane + held_ref[j + 1] * BLOCK], 0)
        at = pl.ds(b, 1)
        ok = (pos >= first_ref[at, :]) & (pos <= own_ref[at, :])
        w = jnp.where(ok, jnp.exp2(s * (SCALE * LOG2E) - norm_ref[at, :]), 0.0)
        ds = (w * (dp - dot_ref[at, :]) * SCALE).astype(jnp.bfloat16)
        dv = jnp.dot(w.astype(jnp.bfloat16), do, preferred_element_type=jnp.float32)
        dk = jnp.dot(ds, q, preferred_element_type=jnp.float32)
        dqt = lax.dot_general(k, ds, TN, preferred_element_type=jnp.float32)
        return b, a0, a1, dqt, dk, dv

    def two(i, carry):
        for b, a0, a1, dqt, dk, dv in [one(2 * i), one(2 * i + 1)]:
            dqt_ref[pl.ds(pl.multiple_of(b * HEAD, HEAD), HEAD), :] += dqt
            acc_ref[pl.ds(a0, BLOCK), :] += dk[:BLOCK]
            acc_ref[pl.ds(a1, BLOCK), :] += dk[BLOCK:]
            acc_ref[pl.ds(a0 + ROWS, BLOCK), :] += dv[:BLOCK]
            acc_ref[pl.ds(a1 + ROWS, BLOCK), :] += dv[BLOCK:]
        return carry

    lax.fori_loop(0, work_ref[2 * SLOTS], two, 0)
    copies = []
    for i in range(4):
        at = pl.ds(i * PEERS * BLOCK, PEERS * BLOCK)
        half_ref[at, :] = acc_ref[at, :].astype(jnp.bfloat16)
        copies.append(pltpu.make_async_copy(half_ref.at[at], dkv_ref.at[at], sem.at[i]))
        copies[-1].start()
    for g in (1, 3, 2, 0):
        buf, to = (side_buf, side_ref) if g % 2 else (keep_buf, (dq0_ref, dq2_ref)[g // 2])
        for i in range(2):
            b = 2 * g + i
            dq = dqt_ref[b * HEAD : (b + 1) * HEAD, :].T.astype(buf.dtype)
            for h in range(HEADS):
                buf[g // 2, i * BLOCK : (i + 1) * BLOCK, head(h)] = dq[h * BLOCK : (h + 1) * BLOCK]
        to = to.at[g // 2] if g % 2 else to
        copies.append(pltpu.make_async_copy(buf.at[g // 2], to, sem.at[4 + g]))
        copies[-1].start()
    for copy in copies:
        copy.wait()


def pass_on(dq_ref, side_ref, out_ref):
    out_ref[...] = (dq_ref[...] + side_ref[1].astype(jnp.float32)).astype(jnp.bfloat16)


def finish(got_ref, own_ref, side_ref, far_ref, dq_ref, k_ref, v_ref):
    f32, bf16 = jnp.float32, jnp.bfloat16
    both = got_ref[0].astype(f32)
    for i in range(1, PEERS):
        both = both + got_ref[i].astype(f32)
    k_ref[...] = both[:ROWS].astype(bf16)
    v_ref[...] = both[ROWS:].astype(bf16)
    parts = side_ref[0].astype(f32) + far_ref[...].astype(f32)
    dq_ref[...] = (own_ref[...] + parts).astype(bf16)


def plan(doc_lengths, block_order, yh, xh, xl, core):
    docs, nblk = doc_lengths.shape[0], block_order.shape[0]
    nheld = nblk // 4
    upto = jnp.arange(docs)[:, None] >= jnp.arange(docs)[None, :]
    ends = jnp.sum(jnp.where(upto, doc_lengths[None, :], 0), axis=1)
    blocks = jnp.arange(nblk, dtype=jnp.int32)
    held_here = ((blocks // 2) % 2 == core) & ((blocks // 4) % 2 == xl)
    place = (blocks // 8) * (2 * ROWS) + (blocks % 2) * BLOCK
    before = held_here[None, :] & (block_order[None, :] < block_order[:, None])
    rank = jnp.sum(before.astype(jnp.int32), axis=1)
    slots = jnp.arange(nheld + 8, dtype=jnp.int32)
    hit = held_here[None, :] & (rank[None, :] == slots[:, None])
    held = jnp.sum(jnp.where(hit, block_order[None, :], 0), axis=1)
    held = jnp.where(slots < nheld, held, nblk)
    place = jnp.sum(jnp.where(hit, place[None, :], 0), axis=1)
    x, turn = 2 * xh + xl, 1 - 2 * core
    owners = 8 * yh + jnp.stack(
        [
            2 * x + core,
            2 * x + 1 - core,
            2 * ((x + turn) % 4) + core,
            2 * ((x - turn) % 4) + 1 - core,
        ]
    )
    stored = (2 * owners[:, None] + jnp.arange(2)[None, :]).reshape(8)
    mine = jnp.sum(jnp.where(stored[:, None] == blocks[None, :], block_order[None, :], 0), axis=1)
    pos = mine[:, None] * BLOCK + jnp.arange(BLOCK, dtype=jnp.int32)[None, :]
    first = jnp.max(jnp.where(ends[None, None, :] <= pos[:, :, None], ends[None, None, :], 0), axis=2)
    begin = jnp.sum((held[None, :] < (first[:, :1] >> 6)).astype(jnp.int32), axis=1)
    until = jnp.sum((held[None, :] <= mine[:, None]).astype(jnp.int32), axis=1)
    pairs = (until - begin + 1) >> 1
    eight = jnp.arange(8)
    stops = jnp.sum(jnp.where(eight[:, None] >= eight[None, :], pairs[None, :], 0), axis=1)
    place_in = jnp.arange(SLOTS, dtype=jnp.int32)
    done = stops[None, :] <= place_in[:, None]
    of = jnp.sum(done.astype(jnp.int32), axis=1)
    this = of[:, None] == eight[None, :]
    at = jnp.sum(jnp.where(this, begin[None, :] - 2 * (stops - pairs)[None, :], 0), axis=1)
    at = jnp.where(of < 8, at + 2 * place_in, nheld)
    work = jnp.concatenate([jnp.minimum(of, 7), at, (stops[-1:] + 1) >> 1])
    return work, held, place, jnp.tile(first, (1, HEADS)), jnp.tile(pos, (1, HEADS))


def on_device(queries, keys, values, attn_out, grad_out, log_norm, doc_lengths, block_order):
    f32, bf16 = jnp.float32, jnp.bfloat16
    shape = jax.ShapeDtypeStruct
    place = [lax.axis_index(a) for a in CTX]
    dma = pltpu.SemaphoreType.DMA

    swap = [(0, 1), (1, 0)]
    there = [(2 * ((i + 1) % 4), 2 * i) for i in range(4)]
    there += [(2 * i + 1, 2 * ((i + 1) % 4) + 1) for i in range(4)]
    back = [(j, i) for i, j in there]
    sent, p0 = call(
        pack,
        (pltpu.HBM((PEERS, 2 * ROWS, HEAD), bf16), shape((2 * ROWS + EXTRA, WIDTH), bf16)),
        [HBM] * 6,
        (HBM, VMEM),
        *map(in_hbm, (keys, values, queries, grad_out, attn_out, log_norm)),
        scratch=[
            pltpu.VMEM((2 * ROWS, HEAD), bf16),
            pltpu.VMEM((ROWS, WIDTH), bf16),
            pltpu.VMEM((HEADS, ROWS), f32),
            dma((6,)),
            dma((PEERS,)),
        ],
    )
    kv = lax.all_to_all(sent, KEEPERS, 0, 0, tiled=True)
    p2 = lax.ppermute(p0, NEXT, there)
    p3 = lax.ppermute(p2, "core", swap)
    work, held, at, first, own = plan(doc_lengths, block_order, *place)
    later, held = lax.optimization_barrier((p0, held))
    p1 = lax.ppermute(later, "core", swap)
    nkeys = 2 * PEERS * ROWS
    dq0, dq2, side, dkv = call(
        terms,
        (pltpu.HBM((ROWS, WIDTH), f32),) * 2
        + (pltpu.HBM((2, ROWS, WIDTH), bf16), pltpu.HBM((nkeys, HEAD), bf16)),
        [SMEM] * 3 + [VMEM] * 7,
        (HBM,) * 4,
        work, held, at, first, own, p0, p1, p2, p3, kv.reshape(nkeys, HEAD),
        scratch=[
            pltpu.VMEM((nkeys, HEAD), f32),
            pltpu.VMEM((nkeys, HEAD), bf16),
            pltpu.VMEM((8 * HEAD, LANES), f32),
            pltpu.VMEM((2, ROWS, WIDTH), f32),
            pltpu.VMEM((2, ROWS, WIDTH), bf16),
            pltpu.VMEM((8 * LANES, HEAD), bf16),
            pltpu.VMEM((8 * LANES, HEAD), bf16),
            pltpu.VMEM((8, LANES), f32),
            pltpu.VMEM((8, LANES), f32),
            dma((8,)),
        ],
    )
    got = lax.all_to_all(dkv.reshape(PEERS, 2 * ROWS, HEAD), KEEPERS, 0, 0, tiled=True)
    side = lax.ppermute(side, "core", swap)
    far = call(pass_on, shape((ROWS, WIDTH), bf16), [VMEM] * 2, VMEM, dq2, side)
    far = lax.ppermute(far, NEXT, back)
    grad_q, grad_k, grad_v = call(
        finish,
        (shape((ROWS, WIDTH), bf16),) + (shape((ROWS, HEAD), bf16),) * 2,
        [VMEM] * 4,
        (VMEM,) * 3,
        got, dq0, side, far,
    )
    return grad_q, grad_k, grad_v


def solution(mesh):
    parts = Mesh(
        mesh.devices.reshape(2, 4, 2, 2, 2, 8), ("dp", "yh", "xh", "xl", "core", "tensor")
    )
    seq = ("dp",) + CTX
    wide = P(seq, "tensor")
    return jax.shard_map(
        on_device,
        mesh=parts,
        in_specs=(wide,) * 5 + (P("tensor", seq), P("dp"), P("dp")),
        out_specs=(wide, wide, wide),
        check_vma=False,
    )
```

```python
import math

import jax
import jax.numpy as jnp
from jax import lax
from jax.experimental import pallas as pl
from jax.experimental.pallas import tpu as pltpu
from jax.sharding import Mesh
from jax.sharding import PartitionSpec as P

HEADS = 8
HEAD = 128
BLOCK = 64
ROWS = 2 * BLOCK
WIDTH = HEADS * HEAD
LANES = HEADS * BLOCK
EXTRA = 16
PEERS = 8
SLOTS = 72
SCALE = 1.0 / math.sqrt(HEAD)
LOG2E = math.log2(math.e)
CTX = ("yh", "xh", "xl", "core")
KEEPERS = ("yh", "xl")
NEXT = ("xh", "xl", "core")
NT = (((1,), (1,)), ((), ()))
TN = (((0,), (0,)), ((), ()))
VMEM = pl.BlockSpec(memory_space=pltpu.VMEM)
SMEM = pl.BlockSpec(memory_space=pltpu.SMEM)
HBM = pl.BlockSpec(memory_space=pltpu.HBM)


def head(h):
    return slice(h * HEAD, (h + 1) * HEAD)


def in_hbm(x):
    return pltpu.with_memory_space_constraint(x, pltpu.HBM)


def call(kernel, out, ins, outs, *args, scratch=(), limit=16):
    return pl.pallas_call(
        kernel,
        out_shape=out,
        in_specs=ins,
        out_specs=outs,
        scratch_shapes=scratch,
        compiler_params=pltpu.CompilerParams(vmem_limit_bytes=limit << 20),
        name=kernel.__name__,
    )(*args)


def terms_of(x):
    parts = []
    for _ in range(3):
        term = x.astype(jnp.bfloat16).astype(jnp.float32)
        parts.append(term)
        x = x - term
    return parts


def pack(
    k_ref, v_ref, q_ref, do_ref, o_ref, norm_ref,
    kv_ref, out_ref, kv_buf, o_buf, norm_buf, sem, kv_sem,
):
    reads = [
        pltpu.make_async_copy(k_ref, kv_buf.at[:ROWS], sem.at[0]),
        pltpu.make_async_copy(v_ref, kv_buf.at[ROWS:], sem.at[1]),
        pltpu.make_async_copy(do_ref, out_ref.at[ROWS : 2 * ROWS], sem.at[2]),
        pltpu.make_async_copy(o_ref, o_buf, sem.at[3]),
        pltpu.make_async_copy(norm_ref, norm_buf, sem.at[4]),
        pltpu.make_async_copy(q_ref, out_ref.at[:ROWS], sem.at[5]),
    ]
    for copy in reads:
        copy.start()
    for copy in reads[:2]:
        copy.wait()
    writes = [pltpu.make_async_copy(kv_buf, kv_ref.at[i], kv_sem.at[i]) for i in range(PEERS)]
    for copy in writes:
        copy.start()
    for copy in reads[2:5]:
        copy.wait()
    ones = jnp.ones((8, HEAD), jnp.bfloat16)
    dots = []
    for b in range(2):
        at = slice(b * BLOCK, (b + 1) * BLOCK)
        at2 = slice(ROWS + b * BLOCK, ROWS + (b + 1) * BLOCK)
        prod = jnp.concatenate(
            [
                out_ref[at2, head(h)].astype(jnp.float32) * o_buf[at, head(h)].astype(jnp.float32)
                for h in range(HEADS)
            ],
            0,
        )
        high = prod.astype(jnp.bfloat16)
        low = (prod - high.astype(jnp.float32)).astype(jnp.bfloat16)
        dots.append(
            lax.dot_general(ones, high, NT, preferred_element_type=jnp.float32)[:1]
            + lax.dot_general(ones, low, NT, preferred_element_type=jnp.float32)[:1]
        )
    norms = terms_of(norm_buf[...])
    norms = jnp.concatenate(norms + [jnp.zeros((8, WIDTH - 3 * HEAD), jnp.float32)], 1)
    dots = terms_of(jnp.concatenate(dots, 1))
    dots = dots + [jnp.zeros((5, WIDTH), jnp.float32)]
    out_ref[2 * ROWS :] = jnp.concatenate([norms] + dots, 0).astype(jnp.bfloat16)
    reads[5].wait()
    for copy in writes:
        copy.wait()


def stage(p_refs, q_ref, do_ref, norm_ref, dot_ref):
    for g, p_ref in enumerate(p_refs):
        more = p_ref[2 * ROWS :, :].astype(jnp.float32)
        norm = (more[:8, head(0)] + more[:8, head(1)] + more[:8, head(2)]) * LOG2E
        turned = pltpu.roll(norm, BLOCK, 1)
        left = lax.broadcasted_iota(jnp.int32, (1, HEAD), 1) < BLOCK
        dots = more[8:9] + more[9:10] + more[10:11]
        for i in range(2):
            b = 2 * g + i
            dot_ref[b : b + 1, :] = dots[:, i * LANES : (i + 1) * LANES]
            one, two = (norm, turned) if i == 0 else (turned, norm)
            for t in range(HEADS // 2):
                norm_ref[b : b + 1, t * HEAD : (t + 1) * HEAD] = jnp.where(
                    left, one[2 * t : 2 * t + 1], two[2 * t + 1 : 2 * t + 2]
                )
            for h in range(HEADS):
                to = slice(b * LANES + h * BLOCK, b * LANES + (h + 1) * BLOCK)
                q_ref[to, :] = p_ref[i * BLOCK : (i + 1) * BLOCK, head(h)]
                do_ref[to, :] = p_ref[ROWS + i * BLOCK : ROWS + (i + 1) * BLOCK, head(h)]


def terms(
    work_ref, held_ref, place_ref, first_ref, own_ref, p0_ref, p1_ref, p2_ref, p3_ref, kv_ref,
    dq0_ref, dq2_ref, side_ref, dkv_ref,
    acc_ref, half_ref, dqt_ref, own_buf, dq2_buf, q_ref, do_ref, norm_ref, dot_ref, sem,
):
    acc_ref[...] = jnp.zeros_like(acc_ref)
    dqt_ref[...] = jnp.zeros_like(dqt_ref)
    stage((p0_ref, p1_ref, p2_ref, p3_ref), q_ref, do_ref, norm_ref, dot_ref)

    def one(t):
        b, j = work_ref[t], work_ref[SLOTS + t]
        a0 = pl.multiple_of(place_ref[j], BLOCK)
        a1 = pl.multiple_of(place_ref[j + 1], BLOCK)
        rows = pl.ds(pl.multiple_of(b * LANES, LANES), LANES)
        q, do = q_ref[rows, :], do_ref[rows, :]
        k = jnp.concatenate([kv_ref[pl.ds(a0, BLOCK), :], kv_ref[pl.ds(a1, BLOCK), :]], 0)
        v = jnp.concatenate(
            [kv_ref[pl.ds(a0 + ROWS, BLOCK), :], kv_ref[pl.ds(a1 + ROWS, BLOCK), :]], 0
        )
        s = lax.dot_general(k, q, NT, preferred_element_type=jnp.float32)
        dp = lax.dot_general(v, do, NT, preferred_element_type=jnp.float32)
        lane = lax.broadcasted_iota(jnp.int32, (BLOCK, LANES), 0)
        pos = jnp.concatenate([lane + held_ref[j] * BLOCK, lane + held_ref[j + 1] * BLOCK], 0)
        at = pl.ds(b, 1)
        ok = (pos >= first_ref[at, :]) & (pos <= own_ref[at, :])
        w = jnp.where(ok, jnp.exp2(s * (SCALE * LOG2E) - norm_ref[at, :]), 0.0)
        ds = (w * (dp - dot_ref[at, :]) * SCALE).astype(jnp.bfloat16)
        dv = jnp.dot(w.astype(jnp.bfloat16), do, preferred_element_type=jnp.float32)
        dk = jnp.dot(ds, q, preferred_element_type=jnp.float32)
        dqt = lax.dot_general(k, ds, TN, preferred_element_type=jnp.float32)
        return b, a0, a1, dqt, dk, dv

    def two(i, carry):
        for b, a0, a1, dqt, dk, dv in [one(2 * i), one(2 * i + 1)]:
            dqt_ref[pl.ds(pl.multiple_of(b * HEAD, HEAD), HEAD), :] += dqt
            acc_ref[pl.ds(a0, BLOCK), :] += dk[:BLOCK]
            acc_ref[pl.ds(a1, BLOCK), :] += dk[BLOCK:]
            acc_ref[pl.ds(a0 + ROWS, BLOCK), :] += dv[:BLOCK]
            acc_ref[pl.ds(a1 + ROWS, BLOCK), :] += dv[BLOCK:]
        return carry

    lax.fori_loop(0, work_ref[2 * SLOTS], two, 0)
    copies = []
    for i in range(4):
        at = pl.ds(i * PEERS * BLOCK, PEERS * BLOCK)
        half_ref[at, :] = acc_ref[at, :].astype(jnp.bfloat16)
        copies.append(pltpu.make_async_copy(half_ref.at[at], dkv_ref.at[at], sem.at[i]))
        copies[-1].start()
    outs = (own_buf, side_ref.at[0], dq2_buf, side_ref.at[1])
    for g in (0, 2, 1, 3):
        out = outs[g]
        for i in range(2):
            b = 2 * g + i
            dq = dqt_ref[b * HEAD : (b + 1) * HEAD, :].T.astype(out.dtype)
            for h in range(HEADS):
                out[i * BLOCK : (i + 1) * BLOCK, head(h)] = dq[h * BLOCK : (h + 1) * BLOCK]
        if g % 2 == 0:
            to = dq2_ref if g else dq0_ref
            copies.append(pltpu.make_async_copy(out, to, sem.at[4 + g]))
            copies[-1].start()
    for copy in copies:
        copy.wait()


def pass_on(dq_ref, side_ref, out_ref):
    out_ref[...] = (dq_ref[...] + side_ref[1].astype(jnp.float32)).astype(jnp.bfloat16)


def finish(got_ref, own_ref, side_ref, far_ref, dq_ref, k_ref, v_ref):
    f32, bf16 = jnp.float32, jnp.bfloat16
    both = got_ref[0].astype(f32)
    for i in range(1, PEERS):
        both = both + got_ref[i].astype(f32)
    k_ref[...] = both[:ROWS].astype(bf16)
    v_ref[...] = both[ROWS:].astype(bf16)
    parts = side_ref[0].astype(f32) + far_ref[...].astype(f32)
    dq_ref[...] = (own_ref[...] + parts).astype(bf16)


def plan(doc_lengths, block_order, yh, xh, xl, core):
    docs, nblk = doc_lengths.shape[0], block_order.shape[0]
    nheld = nblk // 4
    upto = jnp.arange(docs)[:, None] >= jnp.arange(docs)[None, :]
    ends = jnp.sum(jnp.where(upto, doc_lengths[None, :], 0), axis=1)
    blocks = jnp.arange(nblk, dtype=jnp.int32)
    held_here = ((blocks // 2) % 2 == core) & ((blocks // 8) % 2 == xh)
    place = ((blocks // 16) * 2 + (blocks // 4) % 2) * (2 * ROWS) + (blocks % 2) * BLOCK
    before = held_here[None, :] & (block_order[None, :] < block_order[:, None])
    rank = jnp.sum(before.astype(jnp.int32), axis=1)
    slots = jnp.arange(nheld + 8, dtype=jnp.int32)
    hit = held_here[None, :] & (rank[None, :] == slots[:, None])
    held = jnp.sum(jnp.where(hit, block_order[None, :], 0), axis=1)
    held = jnp.where(slots < nheld, held, nblk)
    place = jnp.sum(jnp.where(hit, place[None, :], 0), axis=1)
    x = 2 * xh + xl
    partner = (x + 2 * xl - 1) % 4
    owners = 8 * yh + jnp.stack(
        [2 * x + core, 2 * x + 1 - core, 2 * partner + core, 2 * partner + 1 - core]
    )
    stored = (2 * owners[:, None] + jnp.arange(2)[None, :]).reshape(8)
    mine = jnp.sum(jnp.where(stored[:, None] == blocks[None, :], block_order[None, :], 0), axis=1)
    pos = mine[:, None] * BLOCK + jnp.arange(BLOCK, dtype=jnp.int32)[None, :]
    first = jnp.max(jnp.where(ends[None, None, :] <= pos[:, :, None], ends[None, None, :], 0), axis=2)
    begin = jnp.sum((held[None, :] < (first[:, :1] >> 6)).astype(jnp.int32), axis=1)
    until = jnp.sum((held[None, :] <= mine[:, None]).astype(jnp.int32), axis=1)
    pairs = (until - begin + 1) >> 1
    eight = jnp.arange(8)
    stops = jnp.sum(jnp.where(eight[:, None] >= eight[None, :], pairs[None, :], 0), axis=1)
    place_in = jnp.arange(SLOTS, dtype=jnp.int32)
    done = stops[None, :] <= place_in[:, None]
    of = jnp.sum(done.astype(jnp.int32), axis=1)
    this = of[:, None] == eight[None, :]
    at = jnp.sum(jnp.where(this, begin[None, :] - 2 * (stops - pairs)[None, :], 0), axis=1)
    at = jnp.where(of < 8, at + 2 * place_in, nheld)
    work = jnp.concatenate([jnp.minimum(of, 7), at, (stops[-1:] + 1) >> 1])
    return work, held, place, jnp.tile(first, (1, HEADS)), jnp.tile(pos, (1, HEADS))


def on_device(queries, keys, values, attn_out, grad_out, log_norm, doc_lengths, block_order):
    f32, bf16 = jnp.float32, jnp.bfloat16
    shape = jax.ShapeDtypeStruct
    place = [lax.axis_index(a) for a in CTX]
    dma = pltpu.SemaphoreType.DMA

    swap = [(0, 1), (1, 0)]
    partner = [3, 2, 1, 0]
    facing = [(2 * i + c, 2 * partner[i] + c) for i in range(4) for c in range(2)]
    sent, p0 = call(
        pack,
        (pltpu.HBM((PEERS, 2 * ROWS, HEAD), bf16), shape((2 * ROWS + EXTRA, WIDTH), bf16)),
        [HBM] * 6,
        (HBM, VMEM),
        *map(in_hbm, (keys, values, queries, grad_out, attn_out, log_norm)),
        scratch=[
            pltpu.VMEM((2 * ROWS, HEAD), bf16),
            pltpu.VMEM((ROWS, WIDTH), bf16),
            pltpu.VMEM((HEADS, ROWS), f32),
            dma((6,)),
            dma((PEERS,)),
        ],
    )
    kv = lax.all_to_all(sent, KEEPERS, 0, 0, tiled=True)
    p2 = lax.ppermute(p0, NEXT, facing)
    p3 = lax.ppermute(p2, "core", swap)
    work, held, at, first, own = plan(doc_lengths, block_order, *place)
    later, held = lax.optimization_barrier((p0, held))
    p1 = lax.ppermute(later, "core", swap)
    nkeys = 2 * PEERS * ROWS
    dq0, dq2, side, dkv = call(
        terms,
        (pltpu.HBM((ROWS, WIDTH), f32),) * 2
        + (shape((2, ROWS, WIDTH), bf16), pltpu.HBM((nkeys, HEAD), bf16)),
        [SMEM] * 3 + [VMEM] * 7,
        (HBM, HBM, VMEM, HBM),
        work, held, at, first, own, p0, p1, p2, p3, kv.reshape(nkeys, HEAD),
        scratch=[
            pltpu.VMEM((nkeys, HEAD), f32),
            pltpu.VMEM((nkeys, HEAD), bf16),
            pltpu.VMEM((8 * HEAD, LANES), f32),
            pltpu.VMEM((ROWS, WIDTH), f32),
            pltpu.VMEM((ROWS, WIDTH), f32),
            pltpu.VMEM((8 * LANES, HEAD), bf16),
            pltpu.VMEM((8 * LANES, HEAD), bf16),
            pltpu.VMEM((8, LANES), f32),
            pltpu.VMEM((8, LANES), f32),
            dma((8,)),
        ],
    )
    got = lax.all_to_all(dkv.reshape(PEERS, 2 * ROWS, HEAD), KEEPERS, 0, 0, tiled=True)
    side = lax.ppermute(side, "core", swap)
    far = call(pass_on, shape((ROWS, WIDTH), bf16), [VMEM] * 2, VMEM, dq2, side)
    far = lax.ppermute(far, NEXT, facing)
    grad_q, grad_k, grad_v = call(
        finish,
        (shape((ROWS, WIDTH), bf16),) + (shape((ROWS, HEAD), bf16),) * 2,
        [VMEM] * 4,
        (VMEM,) * 3,
        got, dq0, side, far,
    )
    return grad_q, grad_k, grad_v


def solution(mesh):
    parts = Mesh(
        mesh.devices.reshape(2, 4, 2, 2, 2, 8), ("dp", "yh", "xh", "xl", "core", "tensor")
    )
    seq = ("dp",) + CTX
    wide = P(seq, "tensor")
    return jax.shard_map(
        on_device,
        mesh=parts,
        in_specs=(wide,) * 5 + (P("tensor", seq), P("dp"), P("dp")),
        out_specs=(wide, wide, wide),
        check_vma=False,
    )
```

```python
import math

import jax
import jax.numpy as jnp
from jax import lax
from jax.experimental import pallas as pl
from jax.experimental.pallas import tpu as pltpu
from jax.sharding import Mesh
from jax.sharding import PartitionSpec as P

HEADS = 8
HEAD = 128
BLOCK = 64
ROWS = 2 * BLOCK
WIDTH = HEADS * HEAD
LANES = HEADS * BLOCK
EXTRA = 16
PEERS = 8
SLOTS = 72
SCALE = 1.0 / math.sqrt(HEAD)
LOG2E = math.log2(math.e)
CTX = ("yh", "xh", "xl", "core")
KEEPERS = ("yh", "xl")
NEXT = ("xh", "xl", "core")
NT = (((1,), (1,)), ((), ()))
TN = (((0,), (0,)), ((), ()))
VMEM = pl.BlockSpec(memory_space=pltpu.VMEM)
SMEM = pl.BlockSpec(memory_space=pltpu.SMEM)
HBM = pl.BlockSpec(memory_space=pltpu.HBM)


def head(h):
    return slice(h * HEAD, (h + 1) * HEAD)


def in_hbm(x):
    return pltpu.with_memory_space_constraint(x, pltpu.HBM)


def call(kernel, out, ins, outs, *args, scratch=(), limit=16):
    return pl.pallas_call(
        kernel,
        out_shape=out,
        in_specs=ins,
        out_specs=outs,
        scratch_shapes=scratch,
        compiler_params=pltpu.CompilerParams(vmem_limit_bytes=limit << 20),
        name=kernel.__name__,
    )(*args)


def terms_of(x):
    parts = []
    for _ in range(3):
        term = x.astype(jnp.bfloat16).astype(jnp.float32)
        parts.append(term)
        x = x - term
    return parts


def pack(
    k_ref, v_ref, q_ref, do_ref, o_ref, norm_ref,
    kv_ref, qx_ref, do_out, kv_buf, o_buf, norm_buf, sem, kv_sem,
):
    reads = [
        pltpu.make_async_copy(k_ref, kv_buf.at[:ROWS], sem.at[0]),
        pltpu.make_async_copy(v_ref, kv_buf.at[ROWS:], sem.at[1]),
        pltpu.make_async_copy(do_ref, do_out, sem.at[2]),
        pltpu.make_async_copy(o_ref, o_buf, sem.at[3]),
        pltpu.make_async_copy(norm_ref, norm_buf, sem.at[4]),
        pltpu.make_async_copy(q_ref, qx_ref.at[:ROWS], sem.at[5]),
    ]
    for copy in reads:
        copy.start()
    for copy in reads[:2]:
        copy.wait()
    writes = [pltpu.make_async_copy(kv_buf, kv_ref.at[i], kv_sem.at[i]) for i in range(PEERS)]
    for copy in writes:
        copy.start()
    for copy in reads[2:5]:
        copy.wait()
    ones = jnp.ones((8, HEAD), jnp.bfloat16)
    dots = []
    for b in range(2):
        at = slice(b * BLOCK, (b + 1) * BLOCK)
        prod = jnp.concatenate(
            [
                do_out[at, head(h)].astype(jnp.float32) * o_buf[at, head(h)].astype(jnp.float32)
                for h in range(HEADS)
            ],
            0,
        )
        high = prod.astype(jnp.bfloat16)
        low = (prod - high.astype(jnp.float32)).astype(jnp.bfloat16)
        dots.append(
            lax.dot_general(ones, high, NT, preferred_element_type=jnp.float32)[:1]
            + lax.dot_general(ones, low, NT, preferred_element_type=jnp.float32)[:1]
        )
    norms = terms_of(norm_buf[...])
    norms = jnp.concatenate(norms + [jnp.zeros((8, WIDTH - 3 * HEAD), jnp.float32)], 1)
    dots = terms_of(jnp.concatenate(dots, 1))
    dots = dots + [jnp.zeros((5, WIDTH), jnp.float32)]
    qx_ref[ROWS:] = jnp.concatenate([norms] + dots, 0).astype(jnp.bfloat16)
    reads[5].wait()
    for copy in writes:
        copy.wait()


def stage(qx_refs, grad_refs, q_ref, do_ref, norm_ref, dot_ref):
    for g, (qx_ref, grad_ref) in enumerate(zip(qx_refs, grad_refs)):
        more = qx_ref[ROWS:, :].astype(jnp.float32)
        norm = (more[:8, head(0)] + more[:8, head(1)] + more[:8, head(2)]) * LOG2E
        turned = pltpu.roll(norm, BLOCK, 1)
        left = lax.broadcasted_iota(jnp.int32, (1, HEAD), 1) < BLOCK
        dots = more[8:9] + more[9:10] + more[10:11]
        for i in range(2):
            b = 2 * g + i
            dot_ref[b : b + 1, :] = dots[:, i * LANES : (i + 1) * LANES]
            one, two = (norm, turned) if i == 0 else (turned, norm)
            for t in range(HEADS // 2):
                norm_ref[b : b + 1, t * HEAD : (t + 1) * HEAD] = jnp.where(
                    left, one[2 * t : 2 * t + 1], two[2 * t + 1 : 2 * t + 2]
                )
            for h in range(HEADS):
                to = slice(b * LANES + h * BLOCK, b * LANES + (h + 1) * BLOCK)
                q_ref[to, :] = qx_ref[i * BLOCK : (i + 1) * BLOCK, head(h)]
                do_ref[to, :] = grad_ref[i * BLOCK : (i + 1) * BLOCK, head(h)]


def terms(
    work_ref, held_ref, place_ref, first_ref, own_ref,
    p0_ref, p1_ref, p2_ref, p3_ref, g0_ref, g1_ref, g2_ref, g3_ref, kv_ref,
    dq0_ref, dq2_ref, side_ref, dkv_ref,
    acc_ref, half_ref, dqt_ref, own_buf, dq2_buf, q_ref, do_ref, norm_ref, dot_ref, sem,
):
    acc_ref[...] = jnp.zeros_like(acc_ref)
    dqt_ref[...] = jnp.zeros_like(dqt_ref)
    rows = (p0_ref, p1_ref, p2_ref, p3_ref), (g0_ref, g1_ref, g2_ref, g3_ref)
    stage(*rows, q_ref, do_ref, norm_ref, dot_ref)

    def one(t):
        b, j = work_ref[t], work_ref[SLOTS + t]
        a0 = pl.multiple_of(place_ref[j], BLOCK)
        a1 = pl.multiple_of(place_ref[j + 1], BLOCK)
        rows = pl.ds(pl.multiple_of(b * LANES, LANES), LANES)
        q, do = q_ref[rows, :], do_ref[rows, :]
        k = jnp.concatenate([kv_ref[pl.ds(a0, BLOCK), :], kv_ref[pl.ds(a1, BLOCK), :]], 0)
        v = jnp.concatenate(
            [kv_ref[pl.ds(a0 + ROWS, BLOCK), :], kv_ref[pl.ds(a1 + ROWS, BLOCK), :]], 0
        )
        s = lax.dot_general(k, q, NT, preferred_element_type=jnp.float32)
        dp = lax.dot_general(v, do, NT, preferred_element_type=jnp.float32)
        lane = lax.broadcasted_iota(jnp.int32, (BLOCK, LANES), 0)
        pos = jnp.concatenate([lane + held_ref[j] * BLOCK, lane + held_ref[j + 1] * BLOCK], 0)
        at = pl.ds(b, 1)
        ok = (pos >= first_ref[at, :]) & (pos <= own_ref[at, :])
        w = jnp.where(ok, jnp.exp2(s * (SCALE * LOG2E) - norm_ref[at, :]), 0.0)
        ds = (w * (dp - dot_ref[at, :]) * SCALE).astype(jnp.bfloat16)
        dv = jnp.dot(w.astype(jnp.bfloat16), do, preferred_element_type=jnp.float32)
        dk = jnp.dot(ds, q, preferred_element_type=jnp.float32)
        dqt = lax.dot_general(k, ds, TN, preferred_element_type=jnp.float32)
        return b, a0, a1, dqt, dk, dv

    def two(i, carry):
        for b, a0, a1, dqt, dk, dv in [one(2 * i), one(2 * i + 1)]:
            dqt_ref[pl.ds(pl.multiple_of(b * HEAD, HEAD), HEAD), :] += dqt
            acc_ref[pl.ds(a0, BLOCK), :] += dk[:BLOCK]
            acc_ref[pl.ds(a1, BLOCK), :] += dk[BLOCK:]
            acc_ref[pl.ds(a0 + ROWS, BLOCK), :] += dv[:BLOCK]
            acc_ref[pl.ds(a1 + ROWS, BLOCK), :] += dv[BLOCK:]
        return carry

    lax.fori_loop(0, work_ref[2 * SLOTS], two, 0)
    copies = []
    for i in range(4):
        at = pl.ds(i * PEERS * BLOCK, PEERS * BLOCK)
        half_ref[at, :] = acc_ref[at, :].astype(jnp.bfloat16)
        copies.append(pltpu.make_async_copy(half_ref.at[at], dkv_ref.at[at], sem.at[i]))
        copies[-1].start()
    outs = (own_buf, side_ref.at[0], dq2_buf, side_ref.at[1])
    for g in (0, 2, 1, 3):
        out = outs[g]
        for i in range(2):
            b = 2 * g + i
            dq = dqt_ref[b * HEAD : (b + 1) * HEAD, :].T.astype(out.dtype)
            for h in range(HEADS):
                out[i * BLOCK : (i + 1) * BLOCK, head(h)] = dq[h * BLOCK : (h + 1) * BLOCK]
        if g % 2 == 0:
            to = dq2_ref if g else dq0_ref
            copies.append(pltpu.make_async_copy(out, to, sem.at[4 + g]))
            copies[-1].start()
    for copy in copies:
        copy.wait()


def pass_on(dq_ref, side_ref, out_ref):
    out_ref[...] = (dq_ref[...] + side_ref[1].astype(jnp.float32)).astype(jnp.bfloat16)


def finish(got_ref, own_ref, side_ref, far_ref, dq_ref, k_ref, v_ref):
    f32, bf16 = jnp.float32, jnp.bfloat16
    both = got_ref[0].astype(f32)
    for i in range(1, PEERS):
        both = both + got_ref[i].astype(f32)
    k_ref[...] = both[:ROWS].astype(bf16)
    v_ref[...] = both[ROWS:].astype(bf16)
    parts = side_ref[0].astype(f32) + far_ref[...].astype(f32)
    dq_ref[...] = (own_ref[...] + parts).astype(bf16)


def plan(doc_lengths, block_order, yh, xh, xl, core):
    docs, nblk = doc_lengths.shape[0], block_order.shape[0]
    nheld = nblk // 4
    upto = jnp.arange(docs)[:, None] >= jnp.arange(docs)[None, :]
    ends = jnp.sum(jnp.where(upto, doc_lengths[None, :], 0), axis=1)
    blocks = jnp.arange(nblk, dtype=jnp.int32)
    held_here = ((blocks // 2) % 2 == core) & ((blocks // 8) % 2 == xh)
    place = ((blocks // 16) * 2 + (blocks // 4) % 2) * (2 * ROWS) + (blocks % 2) * BLOCK
    before = held_here[None, :] & (block_order[None, :] < block_order[:, None])
    rank = jnp.sum(before.astype(jnp.int32), axis=1)
    slots = jnp.arange(nheld + 8, dtype=jnp.int32)
    hit = held_here[None, :] & (rank[None, :] == slots[:, None])
    held = jnp.sum(jnp.where(hit, block_order[None, :], 0), axis=1)
    held = jnp.where(slots < nheld, held, nblk)
    place = jnp.sum(jnp.where(hit, place[None, :], 0), axis=1)
    x = 2 * xh + xl
    partner = (x + 2 * xl - 1) % 4
    owners = 8 * yh + jnp.stack(
        [2 * x + core, 2 * x + 1 - core, 2 * partner + core, 2 * partner + 1 - core]
    )
    stored = (2 * owners[:, None] + jnp.arange(2)[None, :]).reshape(8)
    mine = jnp.sum(jnp.where(stored[:, None] == blocks[None, :], block_order[None, :], 0), axis=1)
    pos = mine[:, None] * BLOCK + jnp.arange(BLOCK, dtype=jnp.int32)[None, :]
    first = jnp.max(jnp.where(ends[None, None, :] <= pos[:, :, None], ends[None, None, :], 0), axis=2)
    begin = jnp.sum((held[None, :] < (first[:, :1] >> 6)).astype(jnp.int32), axis=1)
    until = jnp.sum((held[None, :] <= mine[:, None]).astype(jnp.int32), axis=1)
    pairs = (until - begin + 1) >> 1
    eight = jnp.arange(8)
    stops = jnp.sum(jnp.where(eight[:, None] >= eight[None, :], pairs[None, :], 0), axis=1)
    place_in = jnp.arange(SLOTS, dtype=jnp.int32)
    done = stops[None, :] <= place_in[:, None]
    of = jnp.sum(done.astype(jnp.int32), axis=1)
    this = of[:, None] == eight[None, :]
    at = jnp.sum(jnp.where(this, begin[None, :] - 2 * (stops - pairs)[None, :], 0), axis=1)
    at = jnp.where(of < 8, at + 2 * place_in, nheld)
    work = jnp.concatenate([jnp.minimum(of, 7), at, (stops[-1:] + 1) >> 1])
    return work, held, place, jnp.tile(first, (1, HEADS)), jnp.tile(pos, (1, HEADS))


def on_device(queries, keys, values, attn_out, grad_out, log_norm, doc_lengths, block_order):
    f32, bf16 = jnp.float32, jnp.bfloat16
    shape = jax.ShapeDtypeStruct
    place = [lax.axis_index(a) for a in CTX]
    dma = pltpu.SemaphoreType.DMA

    swap = [(0, 1), (1, 0)]
    partner = [3, 2, 1, 0]
    facing = [(2 * i + c, 2 * partner[i] + c) for i in range(4) for c in range(2)]
    sent, *p0 = call(
        pack,
        (pltpu.HBM((PEERS, 2 * ROWS, HEAD), bf16), shape((ROWS + EXTRA, WIDTH), bf16), shape((ROWS, WIDTH), bf16)),
        [HBM] * 6,
        (HBM, VMEM, VMEM),
        *map(in_hbm, (keys, values, queries, grad_out, attn_out, log_norm)),
        scratch=[
            pltpu.VMEM((2 * ROWS, HEAD), bf16),
            pltpu.VMEM((ROWS, WIDTH), bf16),
            pltpu.VMEM((HEADS, ROWS), f32),
            dma((6,)),
            dma((PEERS,)),
        ],
    )
    kv = lax.all_to_all(sent, KEEPERS, 0, 0, tiled=True)
    p2 = [lax.ppermute(p, NEXT, facing) for p in p0]
    p3 = [lax.ppermute(p, "core", swap) for p in p2]
    work, held, at, first, own = plan(doc_lengths, block_order, *place)
    later, held = lax.optimization_barrier((p0, held))
    p1 = [lax.ppermute(p, "core", swap) for p in later]
    nkeys = 2 * PEERS * ROWS
    dq0, dq2, side, dkv = call(
        terms,
        (pltpu.HBM((ROWS, WIDTH), f32),) * 2
        + (shape((2, ROWS, WIDTH), bf16), pltpu.HBM((nkeys, HEAD), bf16)),
        [SMEM] * 3 + [VMEM] * 11,
        (HBM, HBM, VMEM, HBM),
        work, held, at, first, own, *[p[i] for i in (0, 1) for p in (p0, p1, p2, p3)],
        kv.reshape(nkeys, HEAD),
        scratch=[
            pltpu.VMEM((nkeys, HEAD), f32),
            pltpu.VMEM((nkeys, HEAD), bf16),
            pltpu.VMEM((8 * HEAD, LANES), f32),
            pltpu.VMEM((ROWS, WIDTH), f32),
            pltpu.VMEM((ROWS, WIDTH), f32),
            pltpu.VMEM((8 * LANES, HEAD), bf16),
            pltpu.VMEM((8 * LANES, HEAD), bf16),
            pltpu.VMEM((8, LANES), f32),
            pltpu.VMEM((8, LANES), f32),
            dma((8,)),
        ],
    )
    got = lax.all_to_all(dkv.reshape(PEERS, 2 * ROWS, HEAD), KEEPERS, 0, 0, tiled=True)
    side = lax.ppermute(side, "core", swap)
    far = call(pass_on, shape((ROWS, WIDTH), bf16), [VMEM] * 2, VMEM, dq2, side)
    far = lax.ppermute(far, NEXT, facing)
    grad_q, grad_k, grad_v = call(
        finish,
        (shape((ROWS, WIDTH), bf16),) + (shape((ROWS, HEAD), bf16),) * 2,
        [VMEM] * 4,
        (VMEM,) * 3,
        got, dq0, side, far,
    )
    return grad_q, grad_k, grad_v


def solution(mesh):
    parts = Mesh(
        mesh.devices.reshape(2, 4, 2, 2, 2, 8), ("dp", "yh", "xh", "xl", "core", "tensor")
    )
    seq = ("dp",) + CTX
    wide = P(seq, "tensor")
    return jax.shard_map(
        on_device,
        mesh=parts,
        in_specs=(wide,) * 5 + (P("tensor", seq), P("dp"), P("dp")),
        out_specs=(wide, wide, wide),
        check_vma=False,
    )
```

```python
import math

import jax
import jax.numpy as jnp
from jax import lax
from jax.experimental import pallas as pl
from jax.experimental.pallas import tpu as pltpu
from jax.sharding import Mesh
from jax.sharding import PartitionSpec as P

HEADS = 8
HEAD = 128
BLOCK = 64
ROWS = 2 * BLOCK
WIDTH = HEADS * HEAD
LANES = HEADS * BLOCK
EXTRA = 16
PEERS = 8
SLOTS = 72
SCALE = 1.0 / math.sqrt(HEAD)
LOG2E = math.log2(math.e)
CTX = ("yh", "xh", "xl", "core")
KEEPERS = ("yh", "xl")
NEXT = ("xh", "xl", "core")
NT = (((1,), (1,)), ((), ()))
TN = (((0,), (0,)), ((), ()))
VMEM = pl.BlockSpec(memory_space=pltpu.VMEM)
SMEM = pl.BlockSpec(memory_space=pltpu.SMEM)
HBM = pl.BlockSpec(memory_space=pltpu.HBM)


def head(h):
    return slice(h * HEAD, (h + 1) * HEAD)


def in_hbm(x):
    return pltpu.with_memory_space_constraint(x, pltpu.HBM)


def call(kernel, out, ins, outs, *args, scratch=(), limit=16):
    return pl.pallas_call(
        kernel,
        out_shape=out,
        in_specs=ins,
        out_specs=outs,
        scratch_shapes=scratch,
        compiler_params=pltpu.CompilerParams(vmem_limit_bytes=limit << 20),
        name=kernel.__name__,
    )(*args)


def terms_of(x):
    parts = []
    for _ in range(3):
        term = x.astype(jnp.bfloat16).astype(jnp.float32)
        parts.append(term)
        x = x - term
    return parts


def pack(
    k_ref, v_ref, q_ref, do_ref, o_ref, norm_ref,
    kv_ref, out_ref, kv_buf, o_buf, norm_buf, sem, kv_sem,
):
    reads = [
        pltpu.make_async_copy(k_ref, kv_buf.at[:ROWS], sem.at[0]),
        pltpu.make_async_copy(v_ref, kv_buf.at[ROWS:], sem.at[1]),
        pltpu.make_async_copy(do_ref, out_ref.at[ROWS : 2 * ROWS], sem.at[2]),
        pltpu.make_async_copy(o_ref, o_buf, sem.at[3]),
        pltpu.make_async_copy(norm_ref, norm_buf, sem.at[4]),
        pltpu.make_async_copy(q_ref, out_ref.at[:ROWS], sem.at[5]),
    ]
    for copy in reads:
        copy.start()
    for copy in reads[:2]:
        copy.wait()
    writes = [pltpu.make_async_copy(kv_buf, kv_ref.at[i], kv_sem.at[i]) for i in range(PEERS)]
    for copy in writes:
        copy.start()
    for copy in reads[2:5]:
        copy.wait()
    ones = jnp.ones((8, HEAD), jnp.bfloat16)
    dots = []
    for b in range(2):
        at = slice(b * BLOCK, (b + 1) * BLOCK)
        at2 = slice(ROWS + b * BLOCK, ROWS + (b + 1) * BLOCK)
        prod = jnp.concatenate(
            [
                out_ref[at2, head(h)].astype(jnp.float32) * o_buf[at, head(h)].astype(jnp.float32)
                for h in range(HEADS)
            ],
            0,
        )
        high = prod.astype(jnp.bfloat16)
        low = (prod - high.astype(jnp.float32)).astype(jnp.bfloat16)
        dots.append(
            lax.dot_general(ones, high, NT, preferred_element_type=jnp.float32)[:1]
            + lax.dot_general(ones, low, NT, preferred_element_type=jnp.float32)[:1]
        )
    norms = terms_of(norm_buf[...])
    norms = jnp.concatenate(norms + [jnp.zeros((8, WIDTH - 3 * HEAD), jnp.float32)], 1)
    dots = terms_of(jnp.concatenate(dots, 1))
    dots = dots + [jnp.zeros((5, WIDTH), jnp.float32)]
    out_ref[2 * ROWS :] = jnp.concatenate([norms] + dots, 0).astype(jnp.bfloat16)
    reads[5].wait()
    for copy in writes:
        copy.wait()


def stage(p_refs, q_ref, do_ref, norm_ref, dot_ref):
    for g, p_ref in enumerate(p_refs):
        more = p_ref[2 * ROWS :, :].astype(jnp.float32)
        norm = (more[:8, head(0)] + more[:8, head(1)] + more[:8, head(2)]) * LOG2E
        turned = pltpu.roll(norm, BLOCK, 1)
        left = lax.broadcasted_iota(jnp.int32, (1, HEAD), 1) < BLOCK
        dots = more[8:9] + more[9:10] + more[10:11]
        for i in range(2):
            b = 2 * g + i
            dot_ref[b : b + 1, :] = dots[:, i * LANES : (i + 1) * LANES]
            one, two = (norm, turned) if i == 0 else (turned, norm)
            for t in range(HEADS // 2):
                norm_ref[b : b + 1, t * HEAD : (t + 1) * HEAD] = jnp.where(
                    left, one[2 * t : 2 * t + 1], two[2 * t + 1 : 2 * t + 2]
                )
            for h in range(HEADS):
                to = slice(b * LANES + h * BLOCK, b * LANES + (h + 1) * BLOCK)
                q_ref[to, :] = p_ref[i * BLOCK : (i + 1) * BLOCK, head(h)]
                do_ref[to, :] = p_ref[ROWS + i * BLOCK : ROWS + (i + 1) * BLOCK, head(h)]


def terms(
    work_ref, held_ref, place_ref, first_ref, own_ref, p0_ref, p1_ref, p2_ref, p3_ref, kv_ref,
    dq0_ref, dq2_ref, side_ref, dkv_ref,
    acc_ref, half_ref, dqt_ref, own_buf, dq2_buf, q_ref, do_ref, norm_ref, dot_ref, sem,
):
    acc_ref[...] = jnp.zeros_like(acc_ref)
    dqt_ref[...] = jnp.zeros_like(dqt_ref)
    stage((p0_ref, p1_ref, p2_ref, p3_ref), q_ref, do_ref, norm_ref, dot_ref)

    def one(t):
        b, j = work_ref[t], work_ref[SLOTS + t]
        a0 = pl.multiple_of(place_ref[j], BLOCK)
        a1 = pl.multiple_of(place_ref[j + 1], BLOCK)
        rows = pl.ds(pl.multiple_of(b * LANES, LANES), LANES)
        q, do = q_ref[rows, :], do_ref[rows, :]
        k = jnp.concatenate([kv_ref[pl.ds(a0, BLOCK), :], kv_ref[pl.ds(a1, BLOCK), :]], 0)
        v = jnp.concatenate(
            [kv_ref[pl.ds(a0 + ROWS, BLOCK), :], kv_ref[pl.ds(a1 + ROWS, BLOCK), :]], 0
        )
        s = lax.dot_general(k, q, NT, preferred_element_type=jnp.float32)
        dp = lax.dot_general(v, do, NT, preferred_element_type=jnp.float32)
        lane = lax.broadcasted_iota(jnp.int32, (BLOCK, LANES), 0)
        pos = jnp.concatenate([lane + held_ref[j] * BLOCK, lane + held_ref[j + 1] * BLOCK], 0)
        at = pl.ds(b, 1)
        ok = (pos >= first_ref[at, :]) & (pos <= own_ref[at, :])
        w = jnp.where(ok, jnp.exp2(s * (SCALE * LOG2E) - norm_ref[at, :]), 0.0)
        ds = (w * (dp - dot_ref[at, :]) * SCALE).astype(jnp.bfloat16)
        dv = jnp.dot(w.astype(jnp.bfloat16), do, preferred_element_type=jnp.float32)
        dk = jnp.dot(ds, q, preferred_element_type=jnp.float32)
        dqt = lax.dot_general(k, ds, TN, preferred_element_type=jnp.float32)
        return b, a0, a1, dqt, dk, dv

    def two(i, carry):
        for b, a0, a1, dqt, dk, dv in [one(2 * i), one(2 * i + 1)]:
            dqt_ref[pl.ds(pl.multiple_of(b * HEAD, HEAD), HEAD), :] += dqt
            acc_ref[pl.ds(a0, BLOCK), :] += dk[:BLOCK]
            acc_ref[pl.ds(a1, BLOCK), :] += dk[BLOCK:]
            acc_ref[pl.ds(a0 + ROWS, BLOCK), :] += dv[:BLOCK]
            acc_ref[pl.ds(a1 + ROWS, BLOCK), :] += dv[BLOCK:]
        return carry

    lax.fori_loop(0, work_ref[2 * SLOTS], two, 0)
    copies = []
    for i in range(4):
        at = pl.ds(i * PEERS * BLOCK, PEERS * BLOCK)
        half_ref[at, :] = acc_ref[at, :].astype(jnp.bfloat16)
        copies.append(pltpu.make_async_copy(half_ref.at[at], dkv_ref.at[at], sem.at[i]))
        copies[-1].start()
    outs = (own_buf, side_ref.at[0], dq2_buf, side_ref.at[1])
    for g in (0, 2, 1, 3):
        out = outs[g]
        for i in range(2):
            b = 2 * g + i
            dq = dqt_ref[b * HEAD : (b + 1) * HEAD, :].T.astype(out.dtype)
            for h in range(HEADS):
                out[i * BLOCK : (i + 1) * BLOCK, head(h)] = dq[h * BLOCK : (h + 1) * BLOCK]
        if g % 2 == 0:
            to = dq2_ref if g else dq0_ref
            copies.append(pltpu.make_async_copy(out, to, sem.at[4 + g]))
            copies[-1].start()
    for copy in copies:
        copy.wait()


def pass_on(dq_ref, side_ref, out_ref):
    out_ref[...] = (dq_ref[...] + side_ref[1].astype(jnp.float32)).astype(jnp.bfloat16)


def finish(got_ref, own_ref, side_ref, far_ref, dq_ref, k_ref, v_ref):
    f32, bf16 = jnp.float32, jnp.bfloat16
    both = got_ref[0].astype(f32)
    for i in range(1, PEERS):
        both = both + got_ref[i].astype(f32)
    k_ref[...] = both[:ROWS].astype(bf16)
    v_ref[...] = both[ROWS:].astype(bf16)
    parts = side_ref[0].astype(f32) + far_ref[...].astype(f32)
    dq_ref[...] = (own_ref[...] + parts).astype(bf16)


def plan(doc_lengths, block_order, yh, xh, xl, core):
    docs, nblk = doc_lengths.shape[0], block_order.shape[0]
    nheld = nblk // 4
    upto = jnp.arange(docs)[:, None] >= jnp.arange(docs)[None, :]
    ends = jnp.sum(jnp.where(upto, doc_lengths[None, :], 0), axis=1)
    blocks = jnp.arange(nblk, dtype=jnp.int32)
    held_here = ((blocks // 2) % 2 == core) & ((blocks // 8) % 2 == xh)
    place = ((blocks // 16) * 2 + (blocks // 4) % 2) * (2 * ROWS) + (blocks % 2) * BLOCK
    before = held_here[None, :] & (block_order[None, :] < block_order[:, None])
    rank = jnp.sum(before.astype(jnp.int32), axis=1)
    slots = jnp.arange(nheld + 8, dtype=jnp.int32)
    hit = held_here[None, :] & (rank[None, :] == slots[:, None])
    held = jnp.sum(jnp.where(hit, block_order[None, :], 0), axis=1)
    held = jnp.where(slots < nheld, held, nblk)
    place = jnp.sum(jnp.where(hit, place[None, :], 0), axis=1)
    x = 2 * xh + xl
    partner = (x + 2 * xl - 1) % 4
    owners = 8 * yh + jnp.stack(
        [2 * x + core, 2 * x + 1 - core, 2 * partner + core, 2 * partner + 1 - core]
    )
    stored = (2 * owners[:, None] + jnp.arange(2)[None, :]).reshape(8)
    mine = jnp.sum(jnp.where(stored[:, None] == blocks[None, :], block_order[None, :], 0), axis=1)
    pos = mine[:, None] * BLOCK + jnp.arange(BLOCK, dtype=jnp.int32)[None, :]
    first = jnp.max(jnp.where(ends[None, None, :] <= pos[:, :, None], ends[None, None, :], 0), axis=2)
    begin = jnp.sum((held[None, :] < (first[:, :1] >> 6)).astype(jnp.int32), axis=1)
    until = jnp.sum((held[None, :] <= mine[:, None]).astype(jnp.int32), axis=1)
    pairs = (until - begin + 1) >> 1
    eight = jnp.arange(8)
    stops = jnp.sum(jnp.where(eight[:, None] >= eight[None, :], pairs[None, :], 0), axis=1)
    place_in = jnp.arange(SLOTS, dtype=jnp.int32)
    done = stops[None, :] <= place_in[:, None]
    of = jnp.sum(done.astype(jnp.int32), axis=1)
    this = of[:, None] == eight[None, :]
    at = jnp.sum(jnp.where(this, begin[None, :] - 2 * (stops - pairs)[None, :], 0), axis=1)
    at = jnp.where(of < 8, at + 2 * place_in, nheld)
    work = jnp.concatenate([jnp.minimum(of, 7), at, (stops[-1:] + 1) >> 1])
    return work, held, place, jnp.tile(first, (1, HEADS)), jnp.tile(pos, (1, HEADS))


def on_device(queries, keys, values, attn_out, grad_out, log_norm, doc_lengths, block_order):
    f32, bf16 = jnp.float32, jnp.bfloat16
    shape = jax.ShapeDtypeStruct
    place = [lax.axis_index(a) for a in CTX]
    dma = pltpu.SemaphoreType.DMA

    swap = [(0, 1), (1, 0)]
    partner = [3, 2, 1, 0]
    facing = [(2 * i + c, 2 * partner[i] + c) for i in range(4) for c in range(2)]
    sent, p0 = call(
        pack,
        (pltpu.HBM((PEERS, 2 * ROWS, HEAD), bf16), shape((2 * ROWS + EXTRA, WIDTH), bf16)),
        [HBM] * 6,
        (HBM, VMEM),
        *map(in_hbm, (keys, values, queries, grad_out, attn_out, log_norm)),
        scratch=[
            pltpu.VMEM((2 * ROWS, HEAD), bf16),
            pltpu.VMEM((ROWS, WIDTH), bf16),
            pltpu.VMEM((HEADS, ROWS), f32),
            dma((6,)),
            dma((PEERS,)),
        ],
    )
    kv = lax.all_to_all(sent, KEEPERS, 0, 0, tiled=True)
    p2 = lax.ppermute(p0, NEXT, facing)
    p3 = lax.ppermute(p2, "core", swap)
    work, held, at, first, own = plan(doc_lengths, block_order, *place)
    p1 = lax.ppermute(p0, "core", swap)
    nkeys = 2 * PEERS * ROWS
    dq0, dq2, side, dkv = call(
        terms,
        (pltpu.HBM((ROWS, WIDTH), f32),) * 2
        + (shape((2, ROWS, WIDTH), bf16), pltpu.HBM((nkeys, HEAD), bf16)),
        [SMEM] * 3 + [VMEM] * 7,
        (HBM, HBM, VMEM, HBM),
        work, held, at, first, own, p0, p1, p2, p3, kv.reshape(nkeys, HEAD),
        scratch=[
            pltpu.VMEM((nkeys, HEAD), f32),
            pltpu.VMEM((nkeys, HEAD), bf16),
            pltpu.VMEM((8 * HEAD, LANES), f32),
            pltpu.VMEM((ROWS, WIDTH), f32),
            pltpu.VMEM((ROWS, WIDTH), f32),
            pltpu.VMEM((8 * LANES, HEAD), bf16),
            pltpu.VMEM((8 * LANES, HEAD), bf16),
            pltpu.VMEM((8, LANES), f32),
            pltpu.VMEM((8, LANES), f32),
            dma((8,)),
        ],
    )
    got = lax.all_to_all(dkv.reshape(PEERS, 2 * ROWS, HEAD), KEEPERS, 0, 0, tiled=True)
    side = lax.ppermute(side, "core", swap)
    far = call(pass_on, shape((ROWS, WIDTH), bf16), [VMEM] * 2, VMEM, dq2, side)
    far = lax.ppermute(far, NEXT, facing)
    grad_q, grad_k, grad_v = call(
        finish,
        (shape((ROWS, WIDTH), bf16),) + (shape((ROWS, HEAD), bf16),) * 2,
        [VMEM] * 4,
        (VMEM,) * 3,
        got, dq0, side, far,
    )
    return grad_q, grad_k, grad_v


def solution(mesh):
    parts = Mesh(
        mesh.devices.reshape(2, 4, 2, 2, 2, 8), ("dp", "yh", "xh", "xl", "core", "tensor")
    )
    seq = ("dp",) + CTX
    wide = P(seq, "tensor")
    return jax.shard_map(
        on_device,
        mesh=parts,
        in_specs=(wide,) * 5 + (P("tensor", seq), P("dp"), P("dp")),
        out_specs=(wide, wide, wide),
        check_vma=False,
    )
```
